128 devices in a mesh: tm: 8 (over x, core), ctx: 16 (over y, z).
Axes of the slice: x: 4, y: 4, z: 4, core: 2. Of those that a mesh axis runs over, the one named last changes fastest.
Arguments:
- iterate: float32 [8, 2688, 1536], P('tm', 'ctx'), may hold values from -6 to 6
- anchor: float32 [2688, 1536], P('ctx'), may hold values from -6 to 6
- frame_index: int32 [2688], P('ctx'), may hold values from 0 to 15, never falling along the last dimension, each value on 1 to 336 neighbouring positions
- noise_steps: int32 [8, 16], P('tm'), may hold values from 0 to 11
- qkv_weight: bfloat16 [1536, 4608], replicated, may hold values from -0.15625 to 0.15625
- out_weight: bfloat16 [1536, 1536], replicated, may hold values from -0.15625 to 0.15625
- mod_weight: bfloat16 [256, 4608], replicated, may hold values from -0.375 to 0.375
Outputs:
- updated: float32 [8, 2688, 1536], P('tm', 'ctx')
The draws below stay inside these ranges and needn't reach their ends.
Inputs may be any that keep to these rules, and one draw needn't show every extreme that they name: `frame_index`: frame numbers never fall along the sequence; each of the 16 frames holds 1 to 336 tokens.
All inputs are finite; a program needn't handle non-finite values.
Results may differ from the reference program's by a relative error of at most 0.00051.
Values may be sent and summed in bfloat16 or wider, within the bound.
No kernel may reach another device: no remote copies, remote signals or barrier semaphores. Data moves between devices by JAX's collectives and lax.ppermute only.
A program may use at most 192 MiB of HBM per device.

```python
import math
import jax
import jax.numpy as jnp
import numpy as np
from jax import lax

D = 1536
HEADS = 12
HD = 128
FREQ = 256
NSCHED = 12
L = 2688
TSTEPS = 8
NF = 16
FMAX = 336


def with_ends(result, stream_key, smallest, high):
    extent = result.shape
    place = [jax.random.randint(jax.random.fold_in(stream_key, axis), (), 0, extent[axis]) for axis in range(len(extent))]
    result = result.at[tuple(place)].set(smallest)
    longest = extent.index(max(extent))
    place[longest] = (place[longest] + 1) % extent[longest]
    return result.at[tuple(place)].set(high)


def level_of(own_key, dims, shards, smallest, high):
    level, own = 1.0, jax.random.fold_in(own_key, 6)
    for position, parts in shards:
        heights = jnp.exp(jax.random.uniform(jax.random.fold_in(own, position), (parts,), jnp.float32, smallest / len(shards), high / len(shards)))
        level = level * jnp.repeat(heights, dims[position] // parts).reshape([-1 if axis == position else 1 for axis in range(len(dims))])
    return level


def length_profile(count, total, reach, slope):
    weights = [(1 << 20) // math.isqrt(rank ** slope) + 1 for rank in range(2, count + 1)]
    spare, holding = total - reach - (count - 1), [1] * (count - 1)
    while spare > 0:
        candidates = [i for i in range(count - 1) if holding[i] < reach]
        pool, budget = sum([weights[i] for i in candidates]), spare
        for i in candidates:
            extra = min(reach - holding[i], max(1, budget * weights[i] // pool), spare)
            holding[i] = holding[i] + extra
            spare = spare - extra
    return np.array([reach] + holding)


def uneven(own_key, count, total, bound, skew):
    if count == 2:
        one = jax.random.randint(own_key, (), max(1, total - bound), min(bound, total - 1) + 1)
        return jnp.stack([one, total - one])
    lengths = jnp.asarray(length_profile(count, total, bound, skew), jnp.int32)
    couples = (count - 1) // 2
    donor, taker = lengths[1:1 + 2 * couples:2], lengths[2:2 + 2 * couples:2]
    slack = jnp.minimum(donor - 1, bound - taker)
    passed = jax.random.randint(jax.random.fold_in(own_key, 1), (couples,), 0, 1 << 20) % (slack + 1)
    lengths = lengths.at[1:1 + 2 * couples:2].set(donor - passed).at[2:2 + 2 * couples:2].set(taker + passed)
    return lengths[jax.random.permutation(jax.random.fold_in(own_key, 2), count)]


def noise(key, shape, scale, limit, cuts=(), kind=jnp.bfloat16):
    drawn = jax.random.normal(key, shape, jnp.float32) * scale
    if len(cuts) > 0:
        drawn = level_of(key, shape, cuts, -0.22, 0.18) * drawn
    return jnp.clip(drawn, min=-limit, max=limit).astype(kind)


def setup_inputs(seed: int = 0) -> dict:
    arg_keys = jax.random.split(jax.random.key(seed), 8)
    return {
        "iterate": noise(arg_keys[0], (TSTEPS, L, D), 1.0, 6.0, ((0, 8), (1, 16)), jnp.float32),
        "anchor": noise(arg_keys[1], (L, D), 1.0, 6.0, ((0, 16),), jnp.float32),
        "frame_index": jnp.searchsorted(jnp.cumsum(uneven(arg_keys[2], NF, L, FMAX, 0)), jnp.arange(L), side="right").astype(jnp.int32),
        "noise_steps": with_ends(jax.random.randint(arg_keys[3], (TSTEPS, NF), 0, NSCHED), jax.random.fold_in(arg_keys[3], 1), 0, NSCHED - 1).astype(jnp.int32),
        "qkv_weight": noise(arg_keys[4], (D, 3 * D), D ** -0.5, 0.15625),
        "out_weight": noise(arg_keys[5], (D, D), D ** -0.5, 0.15625),
        "mod_weight": noise(arg_keys[6], (FREQ, 3 * D), FREQ ** -0.5, 0.375),
    }


shift_factor = 5.0
norm_eps = 1e-06

def noise_level(level_index):
    fraction = level_index / NSCHED
    return shift_factor * fraction / (1.0 + (shift_factor - 1.0) * fraction)

def frame_terms(steps_row, mod_weight):
    level_float = steps_row.astype(jnp.float32)
    upper = noise_level(level_float + 1.0)
    lower = noise_level(level_float)
    step_size = upper - lower
    half_freq = FREQ // 2
    rates = jnp.exp(-math.log(10000.0) * jnp.arange(half_freq, dtype=jnp.float32) / half_freq)
    angles = (1000.0 * upper)[:, None] * rates[None, :]
    features = jnp.concatenate([jnp.cos(angles), jnp.sin(angles)], axis=1).astype(jnp.bfloat16)
    modulation = jnp.dot(features, mod_weight, preferred_element_type=jnp.float32)
    return (modulation, step_size)

def layer_norm(latent):
    center = latent - lax.optimization_barrier(jnp.mean(latent, axis=-1, keepdims=True))
    spread = lax.optimization_barrier(jnp.mean(center * center, axis=-1, keepdims=True))
    return center * lax.rsqrt(spread + norm_eps)

def head_norm(projected):
    tok_rows = projected.shape[0]
    split = projected.reshape(tok_rows, HEADS, HD)
    scaled = split * lax.rsqrt(lax.optimization_barrier(jnp.mean(split * split, axis=-1, keepdims=True)) + norm_eps)
    return scaled.reshape(tok_rows, D).astype(jnp.bfloat16)

def velocity_drift(latent, steps_row, frame_index, qkv_weight, out_weight, mod_weight):
    modulation, step_size = frame_terms(steps_row, mod_weight)
    tok_mod = modulation[frame_index]
    tok_step = step_size[frame_index]
    shift_part = tok_mod[:, :D]
    scale_part = tok_mod[:, D:2 * D]
    gate_part = tok_mod[:, 2 * D:]
    normed = (layer_norm(latent) * (1.0 + scale_part) + shift_part).astype(jnp.bfloat16)
    projected = jnp.dot(normed, qkv_weight, preferred_element_type=jnp.float32)
    queries = head_norm(projected[:, :D])
    key_rows = head_norm(projected[:, D:2 * D])
    values = projected[:, 2 * D:].astype(jnp.bfloat16)
    query_heads = queries.reshape(L, HEADS, HD).transpose(1, 0, 2)
    key_heads = key_rows.reshape(L, HEADS, HD).transpose(1, 0, 2)
    value_heads = values.reshape(L, HEADS, HD).transpose(1, 0, 2)
    allowed = frame_index[None, :] <= frame_index[:, None]

    def one_head(operands):
        query_one, key_one, value_one = operands
        scores = jnp.dot(query_one, key_one.T, preferred_element_type=jnp.float32) * HD ** (-0.5)
        weights = jnp.where(allowed, jnp.exp(scores), 0.0)
        denominator = lax.optimization_barrier(jnp.sum(weights, axis=-1))
        numerator = jnp.dot(weights.astype(jnp.bfloat16), value_one, preferred_element_type=jnp.float32)
        return (numerator / denominator[:, None]).astype(jnp.bfloat16)
    head_outputs = lax.map(one_head, (query_heads, key_heads, value_heads))
    attended = head_outputs.transpose(1, 0, 2).reshape(L, D)
    branch = jnp.dot(attended, out_weight, preferred_element_type=jnp.float32)
    return -tok_step[:, None] * (latent + gate_part * branch)

def reference(iterate, anchor, frame_index, noise_steps, qkv_weight, out_weight, mod_weight):

    def advance(running, operands):
        latent, steps_row = operands
        running = running + velocity_drift(latent, steps_row, frame_index, qkv_weight, out_weight, mod_weight)
        return (running, running)
    _, partial_sums = lax.scan(advance, jnp.zeros((L, D), jnp.float32), (iterate, noise_steps))
    return anchor[None, :, :] + partial_sums
```

```python
import functools
import math

import jax
import jax.numpy as jnp
from jax import lax
from jax.experimental import pallas as pl
from jax.experimental.pallas import tpu as pltpu
from jax.sharding import PartitionSpec as P

HD = 128
NSCHED = 12
NF = 16
D = 1536
ROWS = 168
PACK = 176
WIDE = 384
QROWS = 4 * ROWS
BIG = 131072.0
AXES = ("tm", "ctx")

shift_factor = 5.0
norm_eps = 1e-06


def place_of(x, c, y, z):
    return ((x % 4) * 2 + c % 2) * 16 + (y % 4) * 4 + z % 4


def pairs(move):
    found = []
    for x in range(4):
        for c in range(2):
            for y in range(4):
                for z in range(4):
                    to = move(x, c, y, z)
                    if to is not None:
                        found.append((place_of(x, c, y, z), place_of(*to)))
    return found


def along(ring, step):
    def move(x, c, y, z):
        if (c == 0) == (ring == "a"):
            return (x, c, y + step, z)
        return (x, c, y, z + step)

    return pairs(move)


def send(value, route):
    return lax.ppermute(value, AXES, route)


def noise_level(level_index):
    fraction = level_index / NSCHED
    return shift_factor * fraction / (1.0 + (shift_factor - 1.0) * fraction)


def frame_features(steps_row):
    level_float = steps_row.astype(jnp.float32)
    upper = noise_level(level_float + 1.0)
    lower = noise_level(level_float)
    half_freq = 128
    rates = jnp.exp(-math.log(10000.0) * jnp.arange(half_freq, dtype=jnp.float32) / half_freq)
    angles = (1000.0 * upper)[:, None] * rates[None, :]
    features = jnp.concatenate([jnp.cos(angles), jnp.sin(angles)], axis=1).astype(jnp.bfloat16)
    return features, upper - lower


def split3(value):
    high = value.astype(jnp.bfloat16)
    rest = value - high.astype(jnp.float32)
    mid = rest.astype(jnp.bfloat16)
    low = (rest - mid.astype(jnp.float32)).astype(jnp.bfloat16)
    return jnp.concatenate([high, mid, low], axis=0)


def pick_rows(frame_col, table):
    rows = frame_col.shape[0]
    column = lax.broadcasted_iota(jnp.int32, (rows, 3 * NF), 1) % NF
    ones = (column == frame_col).astype(jnp.float32).astype(jnp.bfloat16)
    return jnp.dot(ones, split3(table), preferred_element_type=jnp.float32)


def norm_kernel(latent_ref, frame_col_ref, frame_row_ref, feat_ref, mod_ref, out_ref, picked_ref):
    for half in range(2):
        cols = pl.ds(half * D, D)
        table = jnp.dot(feat_ref[...], mod_ref[:, cols], preferred_element_type=jnp.float32)
        picked_ref[:, cols] = pick_rows(frame_col_ref[...], table)

    def block(i, carry):
        rows = pl.ds(pl.multiple_of(i * 24, 8), 24)
        latent = latent_ref[rows, :]
        center = latent - jnp.mean(latent, axis=-1, keepdims=True)
        spread = jnp.mean(center * center, axis=-1, keepdims=True)
        normal = center * lax.rsqrt(spread + norm_eps)
        out = normal * (1.0 + picked_ref[rows, D:]) + picked_ref[rows, :D]
        out_ref[rows, :] = out.astype(jnp.bfloat16)
        return carry

    lax.fori_loop(0, ROWS // 24, block, 0)
    out_ref[ROWS:, :] = jnp.zeros((PACK - ROWS, D), jnp.bfloat16)
    row = lax.broadcasted_iota(jnp.int32, (8, 256), 0)
    frames = jnp.where(row == 0, jnp.broadcast_to(frame_row_ref[...], (8, 256)), 0)
    out_ref[ROWS:, :256] = frames.astype(jnp.float32).astype(jnp.bfloat16)


def whole(shape):
    return pl.BlockSpec(shape, lambda *_: (0,) * len(shape))


def normed_pack(latent, frame_col, frame_row, features, mod_weight):
    return pl.pallas_call(
        norm_kernel,
        grid=(1,),
        in_specs=[
            whole((ROWS, D)),
            whole((ROWS, 1)),
            whole((1, 256)),
            whole((NF, 256)),
            pl.BlockSpec((256, 2 * D), lambda i: (0, 0)),
        ],
        out_specs=whole((PACK, D)),
        out_shape=jax.ShapeDtypeStruct((PACK, D), jnp.bfloat16),
        scratch_shapes=[pltpu.VMEM((ROWS, 2 * D), jnp.float32)],
        cost_estimate=pl.CostEstimate(
            flops=2 * 256 * 3072 * 16, bytes_accessed=4000000, transcendentals=0
        ),
        name="norm",
    )(latent, frame_col, frame_row, features, mod_weight)


def side_kernel(latent_ref, frame_col_ref, gap_ref, feat_ref, mod_ref, lat_ref, gate_ref):
    table = jnp.dot(feat_ref[...], mod_ref[...], preferred_element_type=jnp.float32)
    picked = pick_rows(frame_col_ref[...], table)
    column = lax.broadcasted_iota(jnp.int32, (ROWS, NF), 1)
    gap = jnp.sum(
        jnp.where(column == frame_col_ref[...], gap_ref[...], 0.0), axis=1, keepdims=True
    )
    lat_ref[...] = -gap * latent_ref[...]
    gate_ref[...] = -gap * picked


def side_terms(latent, frame_col, gap, features, mod_weight):
    return pl.pallas_call(
        side_kernel,
        grid=(1,),
        in_specs=[
            whole((ROWS, D)),
            whole((ROWS, 1)),
            whole((1, NF)),
            whole((NF, 256)),
            pl.BlockSpec((256, D), lambda i: (0, 2)),
        ],
        out_specs=[whole((ROWS, D)), whole((ROWS, D))],
        out_shape=[jax.ShapeDtypeStruct((ROWS, D), jnp.float32)] * 2,
        cost_estimate=pl.CostEstimate(
            flops=2 * 256 * 1536 * 16, bytes_accessed=4000000, transcendentals=0
        ),
        name="side",
    )(latent, frame_col, gap, features, mod_weight)


def heads_normed(projected):
    parts = []
    for h in range(3):
        one = projected[:, h * HD : (h + 1) * HD]
        mean = jnp.mean(one * one, axis=-1, keepdims=True)
        parts.append((one * lax.rsqrt(mean + norm_eps)).astype(jnp.bfloat16))
    return jnp.concatenate(parts, axis=1)


def qkv_kernel(place_ref, n0, n1, n2, n3, wq_ref, wk_ref, wv_ref, q_ref, kv_ref, fr_ref):
    row = lax.broadcasted_iota(jnp.int32, (8, 256), 0)
    frames = jnp.zeros((8, 256), jnp.bfloat16)
    for r, piece in enumerate((n0, n1, n2, n3)):
        rows = pl.ds(r * ROWS, ROWS)
        tokens = piece[:ROWS, :]
        q_ref[rows, :] = heads_normed(
            jnp.dot(tokens, wq_ref[...], preferred_element_type=jnp.float32)
        )
        kv_ref[rows, :WIDE] = heads_normed(
            jnp.dot(tokens, wk_ref[...], preferred_element_type=jnp.float32)
        )
        kv_ref[rows, WIDE:] = jnp.dot(
            tokens, wv_ref[...], preferred_element_type=jnp.float32
        ).astype(jnp.bfloat16)
        here = jnp.broadcast_to(piece[ROWS : ROWS + 1, :256].astype(jnp.float32), (8, 256))
        fr_ref[:, r * 256 : (r + 1) * 256] = here.astype(jnp.bfloat16)


def project(place, pieces, qkv_weight):
    spec = pltpu.PrefetchScalarGridSpec(
        num_scalar_prefetch=1,
        grid=(1,),
        in_specs=[whole((PACK, D))] * 4
        + [
            pl.BlockSpec((D, WIDE), lambda i, p: (0, p[0])),
            pl.BlockSpec((D, WIDE), lambda i, p: (0, 4 + p[0])),
            pl.BlockSpec((D, WIDE), lambda i, p: (0, 8 + p[0])),
        ],
        out_specs=[whole((QROWS, WIDE)), whole((QROWS, 2 * WIDE)), whole((8, 1024))],
    )
    return pl.pallas_call(
        qkv_kernel,
        grid_spec=spec,
        out_shape=[
            jax.ShapeDtypeStruct((QROWS, WIDE), jnp.bfloat16),
            jax.ShapeDtypeStruct((QROWS, 2 * WIDE), jnp.bfloat16),
            jax.ShapeDtypeStruct((8, 1024), jnp.bfloat16),
        ],
        cost_estimate=pl.CostEstimate(
            flops=2 * QROWS * D * 3 * WIDE, bytes_accessed=7000000, transcendentals=0
        ),
        name="qkv",
    )(place, *pieces, qkv_weight, qkv_weight, qkv_weight)


def frames_row(fr_ref):
    parts = [fr_ref[0:1, r * 256 : r * 256 + ROWS].astype(jnp.float32) for r in range(4)]
    return parts


def attend_kernel(n_kv, first, last, *refs):
    refs = list(refs)
    q_ref, qf_ref = refs[:2]
    kvs = [(refs[2 + 2 * i], refs[3 + 2 * i]) for i in range(n_kv)]
    rest = refs[2 + 2 * n_kv :]
    if not first:
        num_in, den_in, rest = rest[0], rest[1], rest[2:]
    if last:
        out_ref, qe_ref, ke_ref = rest
    else:
        num_ref, den_ref, qe_ref, ke_ref = rest

    for r in range(4):
        here = qf_ref[0:1, r * 256 : (r + 1) * 256].astype(jnp.float32)
        level = lax.broadcasted_iota(jnp.int32, (HD, 256), 0).astype(jnp.float32)
        later = jnp.where(level > here, -BIG, 0.0)
        qe_ref[pl.ds(r * ROWS, ROWS), :] = later.T[:ROWS].astype(jnp.bfloat16)
    for i, (_, kf_ref) in enumerate(kvs):
        for r in range(4):
            here = kf_ref[0:1, r * 256 : (r + 1) * 256].astype(jnp.float32)
            level = lax.broadcasted_iota(jnp.int32, (HD, 256), 0).astype(jnp.float32)
            same = jnp.where(level == here, 1.0, 0.0)
            ke_ref[pl.ds(i * QROWS + r * ROWS, ROWS), :] = same.T[:ROWS].astype(jnp.bfloat16)

    scale = HD**-0.5 * math.log2(math.e)
    block = QROWS // 2
    for b in range(2):
        rows = pl.ds(b * block, block)
        dens = []
        for h in range(3):
            cols = pl.ds(h * HD, HD)
            vcols = pl.ds(WIDE + h * HD, HD)
            query = jnp.concatenate([q_ref[rows, cols], qe_ref[rows, :]], axis=1)
            num = None if first else num_in[rows, cols]
            den = None if first else den_in[rows, h : h + 1]
            for i, (kv_ref, _) in enumerate(kvs):
                key = jnp.concatenate(
                    [kv_ref[:, cols], ke_ref[pl.ds(i * QROWS, QROWS), :]], axis=1
                )
                scores = lax.dot_general(
                    query, key, (((1,), (1,)), ((), ())), preferred_element_type=jnp.float32
                )
                weights = jnp.exp2(scores * scale)
                total = jnp.sum(weights, axis=1, keepdims=True)
                part = jnp.dot(
                    weights.astype(jnp.bfloat16),
                    kv_ref[:, vcols],
                    preferred_element_type=jnp.float32,
                )
                num = part if num is None else num + part
                den = total if den is None else den + total
            if last:
                out_ref[rows, cols] = (num / den).astype(jnp.bfloat16)
            else:
                num_ref[rows, cols] = num
                dens.append(den)
        if not last:
            lane = lax.broadcasted_iota(jnp.int32, (block, HD), 1)
            den_ref[rows, :] = jnp.where(
                lane == 0, dens[0], jnp.where(lane == 1, dens[1], dens[2])
            )


def attend(query, query_frames, kvs, carried, last):
    n_kv = len(kvs)
    first = carried is None
    args = [query, query_frames]
    specs = [whole((QROWS, WIDE)), whole((8, 1024))]
    for kv, frames in kvs:
        args += [kv, frames]
        specs += [whole((QROWS, 2 * WIDE)), whole((8, 1024))]
    if not first:
        args += list(carried)
        specs += [whole((QROWS, WIDE)), whole((QROWS, HD))]
    if last:
        outs = [jax.ShapeDtypeStruct((QROWS, WIDE), jnp.bfloat16)]
    else:
        outs = [
            jax.ShapeDtypeStruct((QROWS, WIDE), jnp.float32),
            jax.ShapeDtypeStruct((QROWS, HD), jnp.float32),
        ]
    return pl.pallas_call(
        functools.partial(attend_kernel, n_kv, first, last),
        grid=(1,),
        in_specs=specs,
        out_specs=[whole(o.shape) for o in outs],
        out_shape=outs,
        scratch_shapes=[
            pltpu.VMEM((QROWS, HD), jnp.bfloat16),
            pltpu.VMEM((n_kv * QROWS, HD), jnp.bfloat16),
        ],
        cost_estimate=pl.CostEstimate(
            flops=4 * QROWS * QROWS * n_kv * WIDE * 2,
            bytes_accessed=2000000,
            transcendentals=QROWS * QROWS * 3 * n_kv,
        ),
        name=f"attend{n_kv}{int(first)}{int(last)}",
    )(*args)


def out_kernel(place_ref, a0, a1, a2, a3, w0, w1, w2, w3, gate_ref, out_ref):
    branch = jnp.dot(a0[...], w0[...], preferred_element_type=jnp.float32)
    for piece, weight in ((a1, w1), (a2, w2), (a3, w3)):
        branch = branch + jnp.dot(piece[...], weight[...], preferred_element_type=jnp.float32)
    out_ref[...] = gate_ref[...] * branch


def project_out(place, pieces, steps, out_weight, gate):
    def rows_of(step):
        return pl.BlockSpec((WIDE, D), lambda i, p: ((p[0] + step) % 4, 0))

    spec = pltpu.PrefetchScalarGridSpec(
        num_scalar_prefetch=1,
        grid=(1,),
        in_specs=[whole((ROWS, WIDE))] * 4 + [rows_of(s) for s in steps] + [whole((ROWS, D))],
        out_specs=whole((ROWS, D)),
    )
    return pl.pallas_call(
        out_kernel,
        grid_spec=spec,
        out_shape=jax.ShapeDtypeStruct((ROWS, D), jnp.float32),
        cost_estimate=pl.CostEstimate(
            flops=2 * ROWS * D * D, bytes_accessed=7000000, transcendentals=0
        ),
        name="out",
    )(place, *pieces, *([out_weight] * 4), gate)


SWAP = pairs(lambda x, c, y, z: (x, 1 - c, y, z))
ROUND1 = pairs(lambda x, c, y, z: (x ^ 1, c, y, z))
ROUND2 = pairs(lambda x, c, y, z: (3 - x, c, y, z) if x < 2 else None)


def earlier_sum(term, chip, core, wire):
    half = D // 2
    mine = jnp.where(core == 0, term[:, :half], term[:, half:])
    others = jnp.where(core == 0, term[:, half:], term[:, :half])
    beside = send(others, SWAP)
    both = mine + beside
    got = send(both.astype(wire), ROUND1).astype(jnp.float32)
    pair = both + got
    far = send(pair.astype(wire), ROUND2).astype(jnp.float32)
    before = jnp.where(chip % 2 == 1, got, 0.0) + jnp.where(chip >= 2, far, 0.0)
    back = send(before + jnp.where(core == 0, mine, 0.0), SWAP)
    own = before + jnp.where(core == 1, beside, 0.0)
    return jnp.concatenate(
        [jnp.where(core == 0, own, back), jnp.where(core == 0, back, own)], axis=1
    )


def per_device(iterate, anchor, frame_index, noise_steps, qkv_weight, out_weight, mod_weight):
    tm = lax.axis_index("tm")
    ctx = lax.axis_index("ctx")
    chip, core = tm // 2, tm % 2
    place = jnp.where(core == 0, ctx // 4, ctx % 4).astype(jnp.int32)[None]
    latent = iterate[0]
    features, gap = frame_features(noise_steps[0])
    frame_col = frame_index[:, None]
    frame_row = jnp.pad(frame_index, (0, 256 - ROWS))[None, :]
    with jax.named_scope("norm"):
        mine = normed_pack(latent, frame_col, frame_row, features, mod_weight)
    steps = (1, -1, 2)
    with jax.named_scope("ring_a"):
        pieces = [mine] + [send(mine, along("a", s)) for s in steps]
    with jax.named_scope("side"):
        lat, gate = side_terms(latent, frame_col, gap[None, :], features, mod_weight)
        base = anchor + (lat + earlier_sum(lat, chip, core, jnp.float32))
    with jax.named_scope("qkv"):
        query, kv, frames = project(place, pieces, qkv_weight)
    with jax.named_scope("ring_b"):
        near = [(send(kv, along("b", s)), send(frames, along("b", s))) for s in steps]
    with jax.named_scope("attend"):
        state = attend(query, frames, [(kv, frames)], None, False)
        state = attend(query, frames, near[:2], state, False)
        (attended,) = attend(query, frames, near[2:], state, True)
    with jax.named_scope("ring_c"):
        back = [attended[:ROWS]]
        for r, s in enumerate(steps):
            back.append(send(attended[(r + 1) * ROWS : (r + 2) * ROWS], along("a", -s)))
    with jax.named_scope("out"):
        term = project_out(place, back, (0,) + steps, out_weight, gate)
    with jax.named_scope("scan"):
        result = base + (term + earlier_sum(term, chip, core, jnp.bfloat16))
    return result[None]


def solution(mesh):
    placed = (P("tm", "ctx", None), P("ctx", None), P("ctx"), P("tm", None), P(), P(), P())
    return jax.shard_map(
        per_device, mesh=mesh, in_specs=placed, out_specs=P("tm", "ctx", None), check_vma=False
    )
```

```python
import functools
import math

import jax
import jax.numpy as jnp
from jax import lax
from jax.experimental import pallas as pl
from jax.experimental.pallas import tpu as pltpu
from jax.sharding import PartitionSpec as P

HD = 128
NSCHED = 12
NF = 16
D = 1536
ROWS = 168
PACK = 176
WIDE = 384
PAIR = 2 * ROWS
PAIRPACK = PAIR + 8
QROWS = 4 * ROWS
HALF = D // 2
BIG = 131072.0
AXES = ("tm", "ctx")

shift_factor = 5.0
norm_eps = 1e-06
F32 = jnp.float32
BF16 = jnp.bfloat16
VM = pl.BlockSpec(memory_space=pltpu.VMEM)
SM = pl.BlockSpec(memory_space=pltpu.SMEM)
ANY = pl.BlockSpec(memory_space=pl.ANY)


def shaped(*shape, kind=F32):
    return jax.ShapeDtypeStruct(shape, kind)


def call(kernel, args, specs, outs, name, cost, scratch=(), mib=24, out_specs=None):
    flops, moved, exps = cost
    return pl.pallas_call(
        kernel,
        in_specs=specs,
        out_specs=[VM] * len(outs) if out_specs is None else out_specs,
        out_shape=outs,
        scratch_shapes=list(scratch),
        compiler_params=pltpu.CompilerParams(vmem_limit_bytes=mib << 20),
        cost_estimate=pl.CostEstimate(flops=flops, bytes_accessed=moved, transcendentals=exps),
        name=name,
    )(*args)


def place_of(x, c, y, z):
    return ((x % 4) * 2 + c % 2) * 16 + (y % 4) * 4 + z % 4


def pairs(move):
    found = []
    for x in range(4):
        for c in range(2):
            for y in range(4):
                for z in range(4):
                    to = move(x, c, y, z)
                    if to is not None:
                        found.append((place_of(x, c, y, z), place_of(*to)))
    return found


def along(ring, step):
    def move(x, c, y, z):
        if (c == 0) == (ring == "a"):
            return (x, c, y + step, z)
        return (x, c, y, z + step)

    return pairs(move)


def send(value, route):
    return lax.ppermute(value, AXES, route)


def noise_level(level_index):
    fraction = level_index / NSCHED
    return shift_factor * fraction / (1.0 + (shift_factor - 1.0) * fraction)


def frame_features(steps_row):
    level_float = steps_row.astype(F32)
    upper = noise_level(level_float + 1.0)
    lower = noise_level(level_float)
    half_freq = 128
    rates = jnp.exp(-math.log(10000.0) * jnp.arange(half_freq, dtype=F32) / half_freq)
    angles = (1000.0 * upper)[:, None] * rates[None, :]
    features = jnp.concatenate([jnp.cos(angles), jnp.sin(angles)], axis=1).astype(BF16)
    return features, upper - lower


def split3(value):
    high = value.astype(BF16)
    rest = value - high.astype(F32)
    mid = rest.astype(BF16)
    low = (rest - mid.astype(F32)).astype(BF16)
    return jnp.concatenate([high, mid, low], axis=0)


def ones_by_frame(frame_row, rows):
    level = lax.broadcasted_iota(jnp.int32, (128, 256), 0)
    here = jnp.broadcast_to(frame_row, (128, 256))
    hit = jnp.where(jnp.logical_and(level % NF == here, level < rows), 1.0, 0.0)
    return hit.T[:ROWS]


def pick_rows(ones, table):
    return jnp.dot(ones[:, : 3 * NF], split3(table), preferred_element_type=F32)


def norm_kernel(latent_hbm, frame_ref, feat_ref, mod_hbm, out_ref, lat_ref, mod_ref, picked_ref, sems):
    copies = [
        pltpu.make_async_copy(mod_hbm.at[:, pl.ds(i * D, D)], mod_ref.at[i], sems.at[i])
        for i in range(2)
    ]
    copies.append(pltpu.make_async_copy(latent_hbm, lat_ref, sems.at[2]))
    for one in copies:
        one.start()
    ones = ones_by_frame(frame_ref[...], 3 * NF).astype(BF16)
    for half in range(2):
        copies[half].wait()
        table = jnp.dot(feat_ref[...], mod_ref[half], preferred_element_type=F32)
        picked_ref[:, pl.ds(half * D, D)] = pick_rows(ones, table)
    copies[2].wait()

    def block(i, carry):
        rows = pl.ds(pl.multiple_of(i * 24, 8), 24)
        latent = lat_ref[rows, :]
        center = latent - jnp.mean(latent, axis=-1, keepdims=True)
        spread = jnp.mean(center * center, axis=-1, keepdims=True)
        normal = center * lax.rsqrt(spread + norm_eps)
        out = normal * (1.0 + picked_ref[rows, D:]) + picked_ref[rows, :D]
        out_ref[rows, :] = out.astype(BF16)
        return carry

    lax.fori_loop(0, ROWS // 24, block, 0)
    out_ref[ROWS:, :] = jnp.zeros((PACK - ROWS, D), BF16)
    out_ref[ROWS:, :256] = jnp.broadcast_to(frame_ref[...], (8, 256)).astype(F32).astype(BF16)


def normed_pack(latent, frame_row, features, mod_weight):
    return call(
        norm_kernel,
        (latent, frame_row, features, mod_weight),
        [ANY, VM, VM, ANY],
        [shaped(PACK, D, kind=BF16)],
        "norm",
        (30000000, 4000000, 0),
        [
            pltpu.VMEM((ROWS, D), F32),
            pltpu.VMEM((2, 256, D), BF16),
            pltpu.VMEM((ROWS, 2 * D), F32),
            pltpu.SemaphoreType.DMA((3,)),
        ],
    )[0]


def side_kernel(
    where_ref,
    after_hbm,
    latent_hbm,
    frame_ref,
    gap_ref,
    feat_ref,
    mod_hbm,
    qkv_hbm,
    keep_ref,
    give_ref,
    gate_ref,
    w_ref,
    lat_ref,
    mod_ref,
    sems,
):
    place, core = where_ref[0], where_ref[1]
    copies = [
        pltpu.make_async_copy(mod_hbm.at[:, pl.ds(2 * D, D)], mod_ref, sems.at[0]),
        pltpu.make_async_copy(latent_hbm, lat_ref, sems.at[1]),
    ]
    for i in range(3):
        cols = pl.ds(pl.multiple_of(i * D + place * WIDE, 128), WIDE)
        copies.append(
            pltpu.make_async_copy(
                qkv_hbm.at[:, cols], w_ref.at[:, pl.ds(i * WIDE, WIDE)], sems.at[2 + i]
            )
        )
    for one in copies:
        one.start()
    ones = ones_by_frame(frame_ref[...], 3 * NF)
    gap = jnp.sum(ones[:, :NF] * gap_ref[:, :NF], axis=1, keepdims=True)
    copies[0].wait()
    table = jnp.dot(feat_ref[...], mod_ref[...], preferred_element_type=F32)
    gate_ref[...] = -gap * pick_rows(ones.astype(BF16), table)
    copies[1].wait()
    mine = pl.ds(pl.multiple_of(core * HALF, 128), HALF)
    other = pl.ds(pl.multiple_of((1 - core) * HALF, 128), HALF)
    keep_ref[...] = -gap * lat_ref[:, mine]
    give_ref[...] = -gap * lat_ref[:, other]
    for one in copies[2:]:
        one.wait()


def side_terms(where, after, latent, frame_row, gap, features, mod_weight, qkv_weight):
    return call(
        side_kernel,
        (where, after, latent, frame_row, gap, features, mod_weight, qkv_weight),
        [SM, ANY, ANY, VM, VM, VM, ANY, ANY],
        [
            shaped(ROWS, HALF),
            shaped(ROWS, HALF),
            shaped(ROWS, D),
            shaped(D, 3 * WIDE, kind=BF16),
        ],
        "side",
        (30000000, 6000000, 0),
        [
            pltpu.VMEM((ROWS, D), F32),
            pltpu.VMEM((256, D), BF16),
            pltpu.SemaphoreType.DMA((5,)),
        ],
    )


def head_normed(one):
    mean = jnp.mean(one * one, axis=-1, keepdims=True)
    return (one * lax.rsqrt(mean + norm_eps)).astype(BF16)


def qkv_kernel(n0, n1, w_ref, q_ref, kv_ref, tok_ref):
    tok_ref[:ROWS, :] = n0[:ROWS, :]
    tok_ref[ROWS:, :] = n1[:ROWS, :]
    tokens = tok_ref[...]
    for h in range(3):
        cols = pl.ds(h * WIDE, WIDE)
        got = jnp.dot(tokens, w_ref[:, cols], preferred_element_type=F32)
        if h == 2:
            kv_ref[:PAIR, WIDE:] = got.astype(BF16)
            continue
        target = q_ref if h == 0 else kv_ref
        for i in range(3):
            part = pl.ds(i * HD, HD)
            target[:PAIR, part] = head_normed(got[:, i * HD : (i + 1) * HD])
    kv_ref[PAIR:, :256] = n0[ROWS:, :256]
    kv_ref[PAIR:, 256:512] = n1[ROWS:, :256]
    kv_ref[PAIR:, 512:] = jnp.zeros((8, 256), BF16)


def project(n0, n1, weight):
    return call(
        qkv_kernel,
        (n0, n1, weight),
        [VM] * 3,
        [shaped(PAIR, WIDE, kind=BF16), shaped(PAIRPACK, 2 * WIDE, kind=BF16)],
        "qkv",
        (2 * PAIR * D * 3 * WIDE, 5000000, 0),
        [pltpu.VMEM((PAIR, D), BF16)],
    )


def lanes_to_rows(pack_ref, put, make):
    for i in range(2):
        here = pack_ref[PAIR : PAIR + 1, i * 256 : (i + 1) * 256].astype(F32)
        level = lax.broadcasted_iota(jnp.int32, (HD, 256), 0).astype(F32)
        put(i, make(level, here).T[:ROWS].astype(BF16))


def attend_kernel(n_kv, first, last, row0, nrows, *refs):
    refs = list(refs)
    if first:
        q0, q1, kvs, rest = refs[0], refs[1], refs[2 : 2 + n_kv], refs[2 + n_kv :]
        num_ref, den_ref, qx_ref, key_ref, val_ref = rest
        for j, (q_ref, kv_ref) in enumerate(((q0, kvs[0]), (q1, kvs[1]))):
            rows = pl.ds(j * PAIR, PAIR)
            for h in range(3):
                qx_ref[rows, pl.ds(h * 256, HD)] = q_ref[:, pl.ds(h * HD, HD)]

            def put(i, block):
                at = pl.ds(j * PAIR + i * ROWS, ROWS)
                for h in range(3):
                    qx_ref[at, pl.ds(h * 256 + HD, HD)] = block

            lanes_to_rows(kv_ref, put, lambda level, here: jnp.where(level > here, -BIG, 0.0))
    else:
        qx_ref, num_in, den_in, kvs, rest = refs[0], refs[1], refs[2], refs[3 : 3 + n_kv], refs[3 + n_kv :]
        if last:
            outs, (key_ref, val_ref) = rest[:-2], rest[-2:]
        else:
            num_ref, den_ref, key_ref, val_ref = rest

    for j, kv_ref in enumerate(kvs):
        rows = pl.ds(j * PAIR, PAIR)
        for h in range(3):
            key_ref[rows, pl.ds(h * 256, HD)] = kv_ref[:PAIR, pl.ds(h * HD, HD)]
        val_ref[rows, :] = kv_ref[:PAIR, WIDE:]

        def put(i, block):
            at = pl.ds(j * PAIR + i * ROWS, ROWS)
            for h in range(3):
                key_ref[at, pl.ds(h * 256 + HD, HD)] = block

        lanes_to_rows(kv_ref, put, lambda level, here: jnp.where(level == here, 1.0, 0.0))

    scale = HD**-0.5 * math.log2(math.e)
    rows = pl.ds(row0, nrows)
    dens = []
    for h in range(3):
        cols = pl.ds(h * HD, HD)
        wide = pl.ds(h * 256, 256)
        scores = lax.dot_general(
            qx_ref[rows, wide], key_ref[:, wide], (((1,), (1,)), ((), ())),
            preferred_element_type=F32,
        )
        weights = jnp.exp2(scores * scale)
        den = jnp.sum(weights, axis=1, keepdims=True)
        num = jnp.dot(weights.astype(BF16), val_ref[:, cols], preferred_element_type=F32)
        if not first:
            num = num + num_in[rows, cols]
            den = den + den_in[rows, h : h + 1]
        if last:
            done = (num / den).astype(BF16)
            for i, out_ref in enumerate(outs):
                out_ref[:, cols] = done[i * ROWS : (i + 1) * ROWS]
        else:
            num_ref[:, cols] = num
            dens.append(den)
    if not last:
        lane = lax.broadcasted_iota(jnp.int32, (QROWS, HD), 1)
        den_ref[...] = jnp.where(lane == 0, dens[0], jnp.where(lane == 1, dens[1], dens[2]))


def attend(kvs, queries=None, state=None, last=None):
    n_kv = len(kvs)
    first = state is None
    row0, nrows = (0, QROWS) if last is None else last
    args = (list(queries) if first else list(state)) + list(kvs)
    if last is None:
        outs = [shaped(QROWS, WIDE), shaped(QROWS, HD)]
        if first:
            outs.append(shaped(QROWS, 768, kind=BF16))
    else:
        outs = [shaped(ROWS, WIDE, kind=BF16)] * (nrows // ROWS)
    got = call(
        functools.partial(attend_kernel, n_kv, first, last is not None, row0, nrows),
        args,
        [VM] * len(args),
        outs,
        f"attend{n_kv}_{int(first)}_{row0}_{nrows}",
        (4 * nrows * PAIR * n_kv * WIDE * 2, 2000000, nrows * PAIR * 3 * n_kv),
        [
            pltpu.VMEM((n_kv * PAIR, 768), BF16),
            pltpu.VMEM((n_kv * PAIR, WIDE), BF16),
        ],
    )
    if last is not None:
        return got
    return (got[2] if first else state[0], got[0], got[1])


def out_first_kernel(where_ref, a_ref, w_hbm, part_ref, w1, w2, w3, w0, sems):
    place = where_ref[0]
    copies = []
    for i, (step, into) in enumerate(((0, w0), (1, w1), (3, w2), (2, w3))):
        rows = pl.ds(pl.multiple_of(lax.rem(place + step, 4) * WIDE, 128), WIDE)
        copies.append(pltpu.make_async_copy(w_hbm.at[rows, :], into, sems.at[i]))
    for one in copies:
        one.start()
    copies[0].wait()
    part_ref[...] = jnp.dot(a_ref[...], w0[...], preferred_element_type=F32)
    for one in copies[1:]:
        one.wait()


def out_first(where, piece, out_weight):
    return call(
        out_first_kernel,
        (where, piece, out_weight),
        [SM, VM, ANY],
        [shaped(ROWS, D)] + [shaped(WIDE, D, kind=BF16)] * 3,
        "out_first",
        (2 * ROWS * WIDE * D, 5000000, 0),
        [pltpu.VMEM((WIDE, D), BF16), pltpu.SemaphoreType.DMA((4,))],
    )


def out_rest_kernel(where_ref, part_ref, a1, a2, a3, w1, w2, w3, gate_ref, keep_ref, give_ref, term_ref):
    core = where_ref[1]
    branch = part_ref[...]
    for piece, weight in ((a1, w1), (a2, w2), (a3, w3)):
        branch = branch + jnp.dot(piece[...], weight[...], preferred_element_type=F32)
    term_ref[...] = gate_ref[...] * branch
    keep_ref[...] = term_ref[:, pl.ds(pl.multiple_of(core * HALF, 128), HALF)]
    give_ref[...] = term_ref[:, pl.ds(pl.multiple_of((1 - core) * HALF, 128), HALF)]


def out_rest(where, part, pieces, weights, gate):
    return call(
        out_rest_kernel,
        (where, part, *pieces, *weights, gate),
        [SM] + [VM] * 8,
        [shaped(ROWS, HALF), shaped(ROWS, HALF)],
        "out_rest",
        (2 * ROWS * 3 * WIDE * D, 5000000, 0),
        [pltpu.VMEM((ROWS, D), F32)],
    )


def join_kernel(where_ref, base_ref, keep_ref, give_ref, own_ref, back_ref, out_ref):
    core = where_ref[1]
    mine = pl.ds(pl.multiple_of(core * HALF, 128), HALF)
    other = pl.ds(pl.multiple_of((1 - core) * HALF, 128), HALF)
    out_ref[:, mine] = base_ref[:, mine] + (keep_ref[...] + own_ref[...])
    out_ref[:, other] = base_ref[:, other] + (give_ref[...] + back_ref[...])


def join(where, base, keep, give, own, back, name):
    return call(
        join_kernel,
        (where, base, keep, give, own, back),
        [SM] + [VM] * 5,
        [shaped(ROWS, D)],
        name,
        (ROWS * D * 2, 4000000, 0),
    )[0]


SWAP = pairs(lambda x, c, y, z: (x, 1 - c, y, z))
ROUND1 = pairs(lambda x, c, y, z: (x ^ 1, c, y, z))
ROUND2 = pairs(lambda x, c, y, z: (3 - x, c, y, z) if x < 2 else None)


def scan_one(keep, give, wire):
    beside = send(give, SWAP)
    both = keep + beside
    return beside, both, send(both.astype(wire), ROUND1)


def scan_two(both, got, wire):
    return send((both + got.astype(F32)).astype(wire), ROUND2)


def scan_three(keep, beside, got, far, chip, core):
    before = jnp.where(chip % 2 == 1, got.astype(F32), 0.0)
    before = before + jnp.where(chip >= 2, far.astype(F32), 0.0)
    back = send(before + jnp.where(core == 0, keep, 0.0), SWAP)
    return before + jnp.where(core == 1, beside, 0.0), back


def per_device(iterate, anchor, frame_index, noise_steps, qkv_weight, out_weight, mod_weight):
    tm = lax.axis_index("tm")
    ctx = lax.axis_index("ctx")
    chip, core = tm // 2, tm % 2
    place = jnp.where(core == 0, ctx // 4, ctx % 4)
    where = jnp.stack([place, core]).astype(jnp.int32)
    latent = iterate[0]
    features, gap = frame_features(noise_steps[0])
    gap = jnp.pad(gap, (0, 128 - NF))[None, :]
    frame_row = jnp.pad(frame_index, (0, 256 - ROWS))[None, :]
    tie = lax.optimization_barrier

    mine = normed_pack(latent, frame_row, features, mod_weight)
    from_prev = send(mine, along("a", 1))
    from_next = send(mine, along("a", -1))
    from_far = send(mine, along("a", 2))
    lat_keep, lat_give, gate, weight = side_terms(
        where, mine, latent, frame_row, gap, features, mod_weight, qkv_weight
    )
    lat_beside, lat_both, lat_got = scan_one(lat_keep, lat_give, F32)

    q0, kv0 = project(mine, from_prev, weight)
    up0 = send(kv0, along("b", 1))
    down0 = send(kv0, along("b", -1))
    q1, kv1 = project(from_next, from_far, weight)
    down1 = send(kv1, along("b", -1))
    up1 = send(kv1, along("b", 1))
    far0 = send(up0, along("b", 1))

    state = attend([kv0, kv1], queries=(q0, q1))
    state, lat_got = tie((state, lat_got))
    lat_far = scan_two(lat_both, lat_got, F32)
    far1 = send(down1, along("b", -1))
    state = attend([up0, down0], state=state)
    state = attend([up1, down1], state=state)
    state, lat_far = tie((state, lat_far))
    lat_own, lat_back = scan_three(lat_keep, lat_beside, lat_got, lat_far, chip, core)
    a1, a2, a3 = attend([far0, far1], state=state, last=(ROWS, 3 * ROWS))
    b1 = send(a1, along("a", -1))
    b2 = send(a2, along("a", 1))
    b3 = send(a3, along("a", -2))
    (a0,) = attend([far0, far1], state=state, last=(0, ROWS))
    base = join(where, anchor, lat_keep, lat_give, lat_own, lat_back, "base")
    part, w1, w2, w3 = out_first(where, a0, out_weight)
    keep, give = out_rest(where, part, (b1, b2, b3), (w1, w2, w3), gate)
    beside, both, got = scan_one(keep, give, BF16)
    far = scan_two(both, got, BF16)
    own, back = scan_three(keep, beside, got, far, chip, core)
    return join(where, base, keep, give, own, back, "final")[None]


def solution(mesh):
    placed = (P("tm", "ctx", None), P("ctx", None), P("ctx"), P("tm", None), P(), P(), P())
    return jax.shard_map(
        per_device, mesh=mesh, in_specs=placed, out_specs=P("tm", "ctx", None), check_vma=False
    )
```

```python
import functools
import math

import jax
import jax.numpy as jnp
from jax import lax
from jax.experimental import pallas as pl
from jax.experimental.pallas import tpu as pltpu
from jax.sharding import PartitionSpec as P


HD = 128
NSCHED = 12
NF = 16
D = 1536
ROWS = 168
PACK = 176
WIDE = 384
PAIR = 2 * ROWS
PAIRPACK = PAIR + 8
QROWS = 4 * ROWS
HALF = D // 2
BIG = 131072.0
AXES = ("tm", "ctx")

shift_factor = 5.0
norm_eps = 1e-06
F32 = jnp.float32
BF16 = jnp.bfloat16
VM = pl.BlockSpec(memory_space=pltpu.VMEM)
SM = pl.BlockSpec(memory_space=pltpu.SMEM)
ANY = pl.BlockSpec(memory_space=pl.ANY)
HBM = pl.BlockSpec(memory_space=pltpu.HBM)


def shaped(*shape, kind=F32):
    return jax.ShapeDtypeStruct(shape, kind)


def call(kernel, args, specs, outs, cost, scratch=(), mib=24, out_specs=None):
    flops, moved, exps = cost
    return run_kernel(kernel, args, specs, outs, flops, moved, exps, scratch, mib, out_specs)


def run_kernel(kernel, args, specs, outs, flops, moved, exps, scratch, mib, out_specs):
    return pl.pallas_call(
        kernel,
        in_specs=specs,
        out_specs=[VM] * len(outs) if out_specs is None else out_specs,
        out_shape=outs,
        scratch_shapes=list(scratch),
        compiler_params=pltpu.CompilerParams(vmem_limit_bytes=mib << 20),
        cost_estimate=pl.CostEstimate(flops=flops, bytes_accessed=moved, transcendentals=exps),
    )(*args)


def place_of(x, c, y, z):
    return ((x % 4) * 2 + c % 2) * 16 + (y % 4) * 4 + z % 4


def pairs(move):
    found = []
    for x in range(4):
        for c in range(2):
            for y in range(4):
                for z in range(4):
                    to = move(x, c, y, z)
                    if to is not None:
                        found.append((place_of(x, c, y, z), place_of(*to)))
    return found


def along(ring, step):
    def move(x, c, y, z):
        if (c == 0) == (ring == "a"):
            return (x, c, y + step, z)
        return (x, c, y, z + step)

    return pairs(move)


def send(value, route):
    return lax.ppermute(value, AXES, route)


def noise_level(level_index):
    fraction = level_index / NSCHED
    return shift_factor * fraction / (1.0 + (shift_factor - 1.0) * fraction)


def frame_features(steps_row):
    level_float = steps_row.astype(F32)
    upper = noise_level(level_float + 1.0)
    lower = noise_level(level_float)
    half_freq = 128
    rates = jnp.exp(-math.log(10000.0) * jnp.arange(half_freq, dtype=F32) / half_freq)
    angles = (1000.0 * upper)[:, None] * rates[None, :]
    features = jnp.concatenate([jnp.cos(angles), jnp.sin(angles)], axis=1).astype(BF16)
    return features, upper - lower


def split3(value):
    high = value.astype(BF16)
    rest = value - high.astype(F32)
    mid = rest.astype(BF16)
    low = (rest - mid.astype(F32)).astype(BF16)
    return jnp.concatenate([high, mid, low], axis=0)


def ones_by_frame(frame_row, rows):
    level = lax.broadcasted_iota(jnp.int32, (128, 256), 0)
    here = jnp.broadcast_to(frame_row, (128, 256))
    hit = jnp.where(jnp.logical_and(level % NF == here, level < rows), 1.0, 0.0)
    return hit.T[:ROWS]


def pick_rows(ones, table):
    return jnp.dot(ones[:, : 3 * NF], split3(table), preferred_element_type=F32)


def norm_kernel(latent_hbm, frame_ref, feat_ref, mod_hbm, out_ref, lat_ref, mod_ref, picked_ref, sems):
    copies = [
        pltpu.make_async_copy(mod_hbm.at[:, pl.ds(i * D, D)], mod_ref.at[i], sems.at[i])
        for i in range(2)
    ]
    copies.append(pltpu.make_async_copy(latent_hbm, lat_ref, sems.at[2]))
    for one in copies:
        one.start()
    ones = ones_by_frame(frame_ref[...], 3 * NF).astype(BF16)
    for half in range(2):
        copies[half].wait()
        table = jnp.dot(feat_ref[...], mod_ref[half], preferred_element_type=F32)
        picked_ref[:, pl.ds(half * D, D)] = pick_rows(ones, table)
    copies[2].wait()

    def block(i, carry):
        rows = pl.ds(pl.multiple_of(i * 24, 8), 24)
        latent = lat_ref[rows, :]
        center = latent - jnp.mean(latent, axis=-1, keepdims=True)
        spread = jnp.mean(center * center, axis=-1, keepdims=True)
        normal = center * lax.rsqrt(spread + norm_eps)
        out = normal * (1.0 + picked_ref[rows, D:]) + picked_ref[rows, :D]
        out_ref[rows, :] = out.astype(BF16)
        return carry

    lax.fori_loop(0, ROWS // 24, block, 0)
    out_ref[ROWS:, :] = jnp.zeros((PACK - ROWS, D), BF16)
    out_ref[ROWS:, :256] = jnp.broadcast_to(frame_ref[...], (8, 256)).astype(F32).astype(BF16)


def normed_pack(latent, frame_row, features, mod_weight):
    return call(
        norm_kernel,
        (latent, frame_row, features, mod_weight),
        [HBM, VM, VM, HBM],
        [shaped(PACK, D, kind=BF16)],
        (30000000, 4000000, 0),
        [
            pltpu.VMEM((ROWS, D), F32),
            pltpu.VMEM((2, 256, D), BF16),
            pltpu.VMEM((ROWS, 2 * D), F32),
            pltpu.SemaphoreType.DMA((3,)),
        ],
        mib=24,
    )[0]


def side_kernel(
    where_ref,
    after_hbm,
    latent_hbm,
    frame_ref,
    gap_ref,
    feat_ref,
    mod_hbm,
    qkv_hbm,
    keep_ref,
    give_ref,
    gate_ref,
    w_ref,
    lat_ref,
    mod_ref,
    sems,
):
    place, core = where_ref[0], where_ref[1]
    copies = [
        pltpu.make_async_copy(mod_hbm.at[:, pl.ds(2 * D, D)], mod_ref, sems.at[0]),
        pltpu.make_async_copy(latent_hbm, lat_ref, sems.at[1]),
    ]
    for i in range(3):
        cols = pl.ds(pl.multiple_of(i * D + place * WIDE, 128), WIDE)
        copies.append(
            pltpu.make_async_copy(
                qkv_hbm.at[:, cols], w_ref.at[:, pl.ds(i * WIDE, WIDE)], sems.at[2 + i]
            )
        )
    for one in copies:
        one.start()
    ones = ones_by_frame(frame_ref[...], 3 * NF)
    gap = jnp.sum(ones[:, :NF] * gap_ref[:, :NF], axis=1, keepdims=True)
    copies[0].wait()
    table = jnp.dot(feat_ref[...], mod_ref[...], preferred_element_type=F32)
    gate_ref[...] = -gap * pick_rows(ones.astype(BF16), table)
    copies[1].wait()
    mine = pl.ds(pl.multiple_of(core * HALF, 128), HALF)
    other = pl.ds(pl.multiple_of((1 - core) * HALF, 128), HALF)
    keep_ref[...] = -gap * lat_ref[:, mine]
    give_ref[...] = -gap * lat_ref[:, other]
    for one in copies[2:]:
        one.wait()


def side_terms(where, after, latent, frame_row, gap, features, mod_weight, qkv_weight):
    return call(
        side_kernel,
        (where, after, latent, frame_row, gap, features, mod_weight, qkv_weight),
        [SM, ANY, HBM, VM, VM, VM, HBM, HBM],
        [
            shaped(ROWS, HALF),
            shaped(ROWS, HALF),
            shaped(ROWS, D),
            shaped(D, 3 * WIDE, kind=BF16),
        ],
        (30000000, 6000000, 0),
        [
            pltpu.VMEM((ROWS, D), F32),
            pltpu.VMEM((256, D), BF16),
            pltpu.SemaphoreType.DMA((5,)),
        ],
        mib=24,
    )


def head_normed(one):
    mean = jnp.mean(one * one, axis=-1, keepdims=True)
    return (one * lax.rsqrt(mean + norm_eps)).astype(BF16)


def qkv_kernel(n_after, *refs):
    n0, n1, w_ref, q_ref, kv_ref, tok_ref = refs[n_after:]
    tok_ref[:ROWS, :] = n0[:ROWS, :]
    tok_ref[ROWS:, :] = n1[:ROWS, :]
    tokens = tok_ref[...]
    for h in range(3):
        cols = pl.ds(h * WIDE, WIDE)
        got = jnp.dot(tokens, w_ref[:, cols], preferred_element_type=F32)
        if h == 2:
            kv_ref[:PAIR, WIDE:] = got.astype(BF16)
            continue
        target = q_ref if h == 0 else kv_ref
        for i in range(3):
            part = pl.ds(i * HD, HD)
            target[:PAIR, part] = head_normed(got[:, i * HD : (i + 1) * HD])
    kv_ref[PAIR:, :256] = n0[ROWS:, :256]
    kv_ref[PAIR:, 256:512] = n1[ROWS:, :256]
    kv_ref[PAIR:, 512:] = jnp.zeros((8, 256), BF16)


def project(n0, n1, weight, after=()):
    return call(
        functools.partial(qkv_kernel, len(after)),
        (*after, n0, n1, weight),
        [ANY] * len(after) + [VM] * 3,
        [shaped(PAIR, WIDE, kind=BF16), shaped(PAIRPACK, 2 * WIDE, kind=BF16)],
        (2 * PAIR * D * 3 * WIDE, 5000000, 0),
        [pltpu.VMEM((PAIR, D), BF16)],
    )


def lanes_to_rows(pack_ref, put, make):
    for i in range(2):
        here = pack_ref[PAIR : PAIR + 1, i * 256 : (i + 1) * 256].astype(F32)
        level = lax.broadcasted_iota(jnp.int32, (HD, 256), 0).astype(F32)
        put(i, make(level, here).T[:ROWS].astype(BF16))


def attend_kernel(n_after, n_kv, first, last, row0, nrows, *refs):
    refs = list(refs)[n_after:]
    if first:
        q0, q1, kvs, rest = refs[0], refs[1], refs[2 : 2 + n_kv], refs[2 + n_kv :]
        num_ref, den_ref, qx_ref, key_ref, val_ref = rest
        for j, (q_ref, kv_ref) in enumerate(((q0, kvs[0]), (q1, kvs[1]))):
            rows = pl.ds(j * PAIR, PAIR)
            for h in range(3):
                qx_ref[rows, pl.ds(h * 256, HD)] = q_ref[:, pl.ds(h * HD, HD)]

            def put(i, block):
                at = pl.ds(j * PAIR + i * ROWS, ROWS)
                for h in range(3):
                    qx_ref[at, pl.ds(h * 256 + HD, HD)] = block

            lanes_to_rows(kv_ref, put, lambda level, here: jnp.where(level > here, -BIG, 0.0))
    else:
        qx_ref, num_in, den_in, kvs, rest = refs[0], refs[1], refs[2], refs[3 : 3 + n_kv], refs[3 + n_kv :]
        if last:
            outs, (key_ref, val_ref) = rest[:-2], rest[-2:]
        else:
            num_ref, den_ref, key_ref, val_ref = rest

    for j, kv_ref in enumerate(kvs):
        rows = pl.ds(j * PAIR, PAIR)
        for h in range(3):
            key_ref[rows, pl.ds(h * 256, HD)] = kv_ref[:PAIR, pl.ds(h * HD, HD)]
        val_ref[rows, :] = kv_ref[:PAIR, WIDE:]

        def put(i, block):
            at = pl.ds(j * PAIR + i * ROWS, ROWS)
            for h in range(3):
                key_ref[at, pl.ds(h * 256 + HD, HD)] = block

        lanes_to_rows(kv_ref, put, lambda level, here: jnp.where(level == here, 1.0, 0.0))

    scale = HD**-0.5 * math.log2(math.e)
    rows = pl.ds(row0, nrows)
    dens = []
    for h in range(3):
        cols = pl.ds(h * HD, HD)
        wide = pl.ds(h * 256, 256)
        scores = lax.dot_general(
            qx_ref[rows, wide], key_ref[:, wide], (((1,), (1,)), ((), ())),
            preferred_element_type=F32,
        )
        weights = jnp.exp2(scores * scale)
        den = jnp.sum(weights, axis=1, keepdims=True)
        num = jnp.dot(weights.astype(BF16), val_ref[:, cols], preferred_element_type=F32)
        if not first:
            num = num + num_in[rows, cols]
            den = den + den_in[rows, h : h + 1]
        if last:
            done = (num / den).astype(BF16)
            for i, out_ref in enumerate(outs):
                out_ref[:, cols] = done[i * ROWS : (i + 1) * ROWS]
        else:
            num_ref[:, cols] = num
            dens.append(den)
    if not last:
        lane = lax.broadcasted_iota(jnp.int32, (QROWS, HD), 1)
        den_ref[...] = jnp.where(lane == 0, dens[0], jnp.where(lane == 1, dens[1], dens[2]))


def attend(kvs, queries=None, state=None, last=None, after=()):
    n_kv = len(kvs)
    first = state is None
    row0, nrows = (0, QROWS) if last is None else last
    args = (list(queries) if first else list(state)) + list(kvs)
    if last is None:
        outs = [shaped(QROWS, WIDE), shaped(QROWS, HD)]
        if first:
            outs.append(shaped(QROWS, 768, kind=BF16))
    else:
        outs = [shaped(ROWS, WIDE, kind=BF16)] * (nrows // ROWS)
    got = call(
        functools.partial(attend_kernel, len(after), n_kv, first, last is not None, row0, nrows),
        list(after) + args,
        [ANY] * len(after) + [VM] * len(args),
        outs,
        (4 * nrows * PAIR * n_kv * WIDE * 2, 2000000, nrows * PAIR * 3 * n_kv),
        [
            pltpu.VMEM((n_kv * PAIR, 768), BF16),
            pltpu.VMEM((n_kv * PAIR, WIDE), BF16),
        ],
    )
    if last is not None:
        return got
    return (got[2] if first else state[0], got[0], got[1])


def out_rows(where_ref, step):
    return pl.ds(pl.multiple_of(lax.rem(where_ref[0] + step, 4) * WIDE, 128), WIDE)


def out_first_kernel(where_ref, a_ref, w_ref, part_ref):
    part_ref[...] = jnp.dot(a_ref[...], w_ref[out_rows(where_ref, 0), :], preferred_element_type=F32)


def out_first(where, piece, out_weight):
    return call(
        out_first_kernel,
        (where, piece, out_weight),
        [SM, VM, VM],
        [shaped(ROWS, D)],
        (2 * ROWS * WIDE * D, 5000000, 0),
    )[0]


def out_rest_kernel(own, where_ref, after_ref, part_ref, a1, a2, a3, w_ref, gate_ref, term_ref):
    core = where_ref[1]
    half = core if own else 1 - core
    cols = pl.ds(pl.multiple_of(half * HALF, 128), HALF)
    branch = part_ref[:, cols]
    for piece, step in ((a1, 1), (a2, 3), (a3, 2)):
        weight = w_ref[out_rows(where_ref, step), cols]
        branch = branch + jnp.dot(piece[...], weight, preferred_element_type=F32)
    term_ref[...] = gate_ref[:, cols] * branch


def out_rest(own, where, after, part, pieces, out_weight, gate):
    return call(
        functools.partial(out_rest_kernel, own),
        (where, after, part, *pieces, out_weight, gate),
        [SM, ANY] + [VM] * 6,
        [shaped(ROWS, HALF)],
        (ROWS * 3 * WIDE * D, 5000000, 0),
    )[0]


def add_kernel(a_ref, b_ref, after_ref, out_ref, wire_ref):
    total = a_ref[...] + b_ref[...].astype(F32)
    out_ref[...] = total
    wire_ref[...] = total.astype(wire_ref.dtype)


def add_up(a, b, wire, after):
    return call(
        add_kernel,
        (a, b, after),
        [VM, VM, ANY],
        [shaped(ROWS, HALF), shaped(ROWS, HALF, kind=wire)],
        (ROWS * HALF, 2000000, 0),
    )


def before_sum(where_ref, got_ref, far_ref):
    chip = where_ref[2]
    near = jnp.where(lax.rem(chip, 2) == 1, got_ref[...].astype(F32), 0.0)
    return near + jnp.where(chip >= 2, far_ref[...].astype(F32), 0.0)


def back_kernel(where_ref, after_ref, keep_ref, got_ref, far_ref, out_ref):
    extra = jnp.where(where_ref[1] == 0, keep_ref[...], 0.0)
    out_ref[...] = before_sum(where_ref, got_ref, far_ref) + extra


def back_sum(where, after, keep, got, far):
    return call(
        back_kernel,
        (where, after, keep, got, far),
        [SM, ANY] + [VM] * 3,
        [shaped(ROWS, HALF)],
        (ROWS * HALF, 2000000, 0),
    )[0]


def join_kernel(where_ref, base_ref, keep_ref, give_ref, beside_ref, got_ref, far_ref, back_ref, out_ref):
    core = where_ref[1]
    mine = pl.ds(pl.multiple_of(core * HALF, 128), HALF)
    other = pl.ds(pl.multiple_of((1 - core) * HALF, 128), HALF)
    own = before_sum(where_ref, got_ref, far_ref) + jnp.where(core == 1, beside_ref[...], 0.0)
    out_ref[:, mine] = base_ref[:, mine] + (keep_ref[...] + own)
    out_ref[:, other] = base_ref[:, other] + (give_ref[...] + back_ref[...])


def join(where, base, keep, give, beside, got, far, back):
    return call(
        join_kernel,
        (where, base, keep, give, beside, got, far, back),
        [SM] + [VM] * 7,
        [shaped(ROWS, D)],
        (ROWS * D * 2, 4000000, 0),
    )[0]


SWAP = pairs(lambda x, c, y, z: (x, 1 - c, y, z))
ROUND1 = pairs(lambda x, c, y, z: (x ^ 1, c, y, z))
ROUND2 = pairs(lambda x, c, y, z: (3 - x, c, y, z) if x < 2 else None)


def held(x):
    return pltpu.with_memory_space_constraint(x, pltpu.HBM)


def per_device(iterate, anchor, frame_index, noise_steps, qkv_weight, out_weight, mod_weight):
    qkv_weight, mod_weight = held(qkv_weight), held(mod_weight)
    tm = lax.axis_index("tm")
    ctx = lax.axis_index("ctx")
    chip, core = tm // 2, tm % 2
    place = jnp.where(core == 0, ctx // 4, ctx % 4)
    where = jnp.stack([place, core, chip]).astype(jnp.int32)
    latent = held(iterate[0])
    features, gap = frame_features(noise_steps[0])
    gap = jnp.pad(gap, (0, 128 - NF))[None, :]
    frame_row = jnp.pad(frame_index, (0, 256 - ROWS))[None, :]

    mine = normed_pack(latent, frame_row, features, mod_weight)
    from_prev = send(mine, along("a", 1))
    from_next = send(mine, along("a", -1))
    from_far = send(mine, along("a", 2))
    lat_keep, lat_give, gate, weight = side_terms(
        where, mine, latent, frame_row, gap, features, mod_weight, qkv_weight
    )
    lat_beside = send(lat_give, SWAP)

    q0, kv0 = project(mine, from_prev, weight)
    up0 = send(kv0, along("b", 1))
    down0 = send(kv0, along("b", -1))
    lat_both, lat_wire = add_up(lat_keep, lat_beside, F32, kv0)
    lat_got = send(lat_wire, ROUND1)
    q1, kv1 = project(from_next, from_far, weight, after=(kv0, lat_wire))
    down1 = send(kv1, along("b", -1))
    up1 = send(kv1, along("b", 1))
    far0 = send(up0, along("b", 1))
    state = attend([kv0, kv1], queries=(q0, q1))
    state = attend([up0, down0], state=state)
    far1 = send(down1, along("b", -1))
    _, lat_wire = add_up(lat_both, lat_got, F32, state[1])
    lat_far = send(lat_wire, ROUND2)
    state = attend([up1, down1], state=state, after=(lat_wire,))
    a1, a2, a3 = attend([far0, far1], state=state, last=(ROWS, 3 * ROWS))
    b3 = send(a3, along("a", -2))
    b1 = send(a1, along("a", -1))
    b2 = send(a2, along("a", 1))
    (a0,) = attend([far0, far1], state=state, last=(0, ROWS), after=(a1,))
    lat_sum = back_sum(where, a0, lat_keep, lat_got, lat_far)
    lat_back = send(lat_sum, SWAP)
    part = out_first(where, a0, out_weight)
    base = join(where, anchor, lat_keep, lat_give, lat_beside, lat_got, lat_far, lat_back)
    pieces = (b1, b2, b3)
    give = out_rest(False, where, base, part, pieces, out_weight, gate)
    beside = send(give, SWAP)
    keep = out_rest(True, where, give, part, pieces, out_weight, gate)
    both, wire = add_up(keep, beside, BF16, keep)
    got = send(wire, ROUND1)
    _, wire = add_up(both, got, BF16, keep)
    far = send(wire, ROUND2)
    back = send(back_sum(where, far, keep, got, far), SWAP)
    return join(where, base, keep, give, beside, got, far, back)[None]


def solution(mesh):
    placed = (P("tm", "ctx", None), P("ctx", None), P("ctx"), P("tm", None), P(), P(), P())

    return jax.shard_map(
        per_device, mesh=mesh, in_specs=placed, out_specs=P("tm", "ctx", None), check_vma=False
    )
```

```python
import functools
import math

import jax
import jax.numpy as jnp
from jax import lax
from jax.experimental import pallas as pl
from jax.experimental.pallas import tpu as pltpu
from jax.sharding import PartitionSpec as P


HD = 128
NSCHED = 12
NF = 16
D = 1536
ROWS = 168
PACK = 176
WIDE = 384
PAIR = 2 * ROWS
PAIRPACK = PAIR + 8
QROWS = 4 * ROWS
HALF = D // 2
BIG = 131072.0
AXES = ("tm", "ctx")

shift_factor = 5.0
norm_eps = 1e-06
F32 = jnp.float32
BF16 = jnp.bfloat16
VM = pl.BlockSpec(memory_space=pltpu.VMEM)
SM = pl.BlockSpec(memory_space=pltpu.SMEM)
ANY = pl.BlockSpec(memory_space=pl.ANY)
HBM = pl.BlockSpec(memory_space=pltpu.HBM)


def shaped(*shape, kind=F32):
    return jax.ShapeDtypeStruct(shape, kind)


def call(kernel, args, specs, outs, cost, scratch=(), mib=24, out_specs=None):
    flops, moved, exps = cost
    return run_kernel(kernel, args, specs, outs, flops, moved, exps, scratch, mib, out_specs)


def run_kernel(kernel, args, specs, outs, flops, moved, exps, scratch, mib, out_specs):
    return pl.pallas_call(
        kernel,
        in_specs=specs,
        out_specs=[VM] * len(outs) if out_specs is None else out_specs,
        out_shape=outs,
        scratch_shapes=list(scratch),
        compiler_params=pltpu.CompilerParams(vmem_limit_bytes=mib << 20),
        cost_estimate=pl.CostEstimate(flops=flops, bytes_accessed=moved, transcendentals=exps),
    )(*args)


def place_of(x, c, y, z):
    return ((x % 4) * 2 + c % 2) * 16 + (y % 4) * 4 + z % 4


def pairs(move):
    found = []
    for x in range(4):
        for c in range(2):
            for y in range(4):
                for z in range(4):
                    to = move(x, c, y, z)
                    if to is not None:
                        found.append((place_of(x, c, y, z), place_of(*to)))
    return found


def along(ring, step):
    def move(x, c, y, z):
        if (c == 0) == (ring == "a"):
            return (x, c, y + step, z)
        return (x, c, y, z + step)

    return pairs(move)


def send(value, route):
    return lax.ppermute(value, AXES, route)


def noise_level(level_index):
    fraction = level_index / NSCHED
    return shift_factor * fraction / (1.0 + (shift_factor - 1.0) * fraction)


def frame_features(steps_row):
    level_float = steps_row.astype(F32)
    upper = noise_level(level_float + 1.0)
    lower = noise_level(level_float)
    half_freq = 128
    rates = jnp.exp(-math.log(10000.0) * jnp.arange(half_freq, dtype=F32) / half_freq)
    angles = (1000.0 * upper)[:, None] * rates[None, :]
    features = jnp.concatenate([jnp.cos(angles), jnp.sin(angles)], axis=1).astype(BF16)
    return features, upper - lower


def split3(value):
    high = value.astype(BF16)
    rest = value - high.astype(F32)
    mid = rest.astype(BF16)
    low = (rest - mid.astype(F32)).astype(BF16)
    return jnp.concatenate([high, mid, low], axis=0)


def ones_by_frame(frame_row, rows):
    level = lax.broadcasted_iota(jnp.int32, (128, 256), 0)
    here = jnp.broadcast_to(frame_row, (128, 256))
    hit = jnp.where(jnp.logical_and(level % NF == here, level < rows), 1.0, 0.0)
    return hit.T[:ROWS]


def pick_rows(ones, table):
    return jnp.dot(ones[:, : 3 * NF], split3(table), preferred_element_type=F32)


def norm_kernel(latent_hbm, frame_ref, feat_ref, mod_hbm, out_ref, lat_ref, mod_ref, picked_ref, sems):
    copies = [
        pltpu.make_async_copy(mod_hbm.at[:, pl.ds(i * D, D)], mod_ref.at[i], sems.at[i])
        for i in range(2)
    ]
    copies.append(pltpu.make_async_copy(latent_hbm, lat_ref, sems.at[2]))
    for one in copies:
        one.start()
    ones = ones_by_frame(frame_ref[...], 3 * NF).astype(BF16)
    for half in range(2):
        copies[half].wait()
        table = jnp.dot(feat_ref[...], mod_ref[half], preferred_element_type=F32)
        picked_ref[:, pl.ds(half * D, D)] = pick_rows(ones, table)
    copies[2].wait()

    def block(i, carry):
        rows = pl.ds(pl.multiple_of(i * 24, 8), 24)
        latent = lat_ref[rows, :]
        center = latent - jnp.mean(latent, axis=-1, keepdims=True)
        spread = jnp.mean(center * center, axis=-1, keepdims=True)
        normal = center * lax.rsqrt(spread + norm_eps)
        out = normal * (1.0 + picked_ref[rows, D:]) + picked_ref[rows, :D]
        out_ref[rows, :] = out.astype(BF16)
        return carry

    lax.fori_loop(0, ROWS // 24, block, 0)
    out_ref[ROWS:, :] = jnp.zeros((PACK - ROWS, D), BF16)
    out_ref[ROWS:, :256] = jnp.broadcast_to(frame_ref[...], (8, 256)).astype(F32).astype(BF16)


def normed_pack(latent, frame_row, features, mod_weight):
    return call(
        norm_kernel,
        (latent, frame_row, features, mod_weight),
        [HBM, VM, VM, HBM],
        [shaped(PACK, D, kind=BF16), shaped(ROWS, D)],
        (30000000, 4000000, 0),
        [
            pltpu.VMEM((2, 256, D), BF16),
            pltpu.VMEM((ROWS, 2 * D), F32),
            pltpu.SemaphoreType.DMA((3,)),
        ],
    )


def frame_gap(ones, gap_ref):
    return jnp.sum(ones[:, :NF] * gap_ref[:, :NF], axis=1, keepdims=True)


def lat_kernel(where_ref, latent_ref, frame_ref, gap_ref, keep_ref, give_ref):
    core = where_ref[1]
    gap = frame_gap(ones_by_frame(frame_ref[...], NF), gap_ref)
    mine = pl.ds(pl.multiple_of(core * HALF, 128), HALF)
    other = pl.ds(pl.multiple_of((1 - core) * HALF, 128), HALF)
    keep_ref[...] = -gap * latent_ref[:, mine]
    give_ref[...] = -gap * latent_ref[:, other]


def lat_terms(where, latent, frame_row, gap):
    return call(
        lat_kernel,
        (where, latent, frame_row, gap),
        [SM, VM, VM, VM],
        [shaped(ROWS, HALF), shaped(ROWS, HALF)],
        (ROWS * D, 2000000, 0),
    )


def side_kernel(
    where_ref, after_ref, frame_ref, gap_ref, feat_ref, mod_hbm, qkv_hbm, gate_ref, w_ref, mod_ref, sems
):
    place = where_ref[0]
    copies = [pltpu.make_async_copy(mod_hbm.at[:, pl.ds(2 * D, D)], mod_ref, sems.at[0])]
    for i in range(3):
        cols = pl.ds(pl.multiple_of(i * D + place * WIDE, 128), WIDE)
        copies.append(
            pltpu.make_async_copy(
                qkv_hbm.at[:, cols], w_ref.at[:, pl.ds(i * WIDE, WIDE)], sems.at[1 + i]
            )
        )
    for one in copies:
        one.start()
    ones = ones_by_frame(frame_ref[...], 3 * NF)
    gap = frame_gap(ones, gap_ref)
    copies[0].wait()
    table = jnp.dot(feat_ref[...], mod_ref[...], preferred_element_type=F32)
    gate_ref[...] = -gap * pick_rows(ones.astype(BF16), table)
    for one in copies[1:]:
        one.wait()


def side_terms(where, after, frame_row, gap, features, mod_weight, qkv_weight):
    return call(
        side_kernel,
        (where, after, frame_row, gap, features, mod_weight, qkv_weight),
        [SM, ANY, VM, VM, VM, HBM, HBM],
        [shaped(ROWS, D), shaped(D, 3 * WIDE, kind=BF16)],
        (30000000, 6000000, 0),
        [pltpu.VMEM((256, D), BF16), pltpu.SemaphoreType.DMA((4,))],
    )


def head_normed(one):
    mean = jnp.mean(one * one, axis=-1, keepdims=True)
    return (one * lax.rsqrt(mean + norm_eps)).astype(BF16)


def qkv_kernel(n_after, *refs):
    n0, n1, w_ref, q_ref, kv_ref, tok_ref = refs[n_after:]
    tok_ref[:ROWS, :] = n0[:ROWS, :]
    tok_ref[ROWS:, :] = n1[:ROWS, :]
    tokens = tok_ref[...]
    for h in range(3):
        cols = pl.ds(h * WIDE, WIDE)
        got = jnp.dot(tokens, w_ref[:, cols], preferred_element_type=F32)
        if h == 2:
            kv_ref[:PAIR, WIDE:] = got.astype(BF16)
            continue
        target = q_ref if h == 0 else kv_ref
        for i in range(3):
            part = pl.ds(i * HD, HD)
            target[:PAIR, part] = head_normed(got[:, i * HD : (i + 1) * HD])
    kv_ref[PAIR:, :256] = n0[ROWS:, :256]
    kv_ref[PAIR:, 256:512] = n1[ROWS:, :256]
    kv_ref[PAIR:, 512:] = jnp.zeros((8, 256), BF16)


def project(n0, n1, weight, after=()):
    return call(
        functools.partial(qkv_kernel, len(after)),
        (*after, n0, n1, weight),
        [ANY] * len(after) + [VM] * 3,
        [shaped(PAIR, WIDE, kind=BF16), shaped(PAIRPACK, 2 * WIDE, kind=BF16)],
        (2 * PAIR * D * 3 * WIDE, 5000000, 0),
        [pltpu.VMEM((PAIR, D), BF16)],
    )


def lanes_to_rows(pack_ref, put, make):
    for i in range(2):
        here = pack_ref[PAIR : PAIR + 1, i * 256 : (i + 1) * 256].astype(F32)
        level = lax.broadcasted_iota(jnp.int32, (HD, 256), 0).astype(F32)
        put(i, make(level, here).T[:ROWS].astype(BF16))


def attend_kernel(n_after, n_kv, first, last, row0, nrows, *refs):
    refs = list(refs)[n_after:]
    if first:
        q0, q1, kvs, rest = refs[0], refs[1], refs[2 : 2 + n_kv], refs[2 + n_kv :]
        num_ref, den_ref, qx_ref, key_ref, val_ref = rest
        for j, (q_ref, kv_ref) in enumerate(((q0, kvs[0]), (q1, kvs[1]))):
            rows = pl.ds(j * PAIR, PAIR)
            for h in range(3):
                qx_ref[rows, pl.ds(h * 256, HD)] = q_ref[:, pl.ds(h * HD, HD)]

            def put(i, block):
                at = pl.ds(j * PAIR + i * ROWS, ROWS)
                for h in range(3):
                    qx_ref[at, pl.ds(h * 256 + HD, HD)] = block

            lanes_to_rows(kv_ref, put, lambda level, here: jnp.where(level > here, -BIG, 0.0))
    else:
        qx_ref, num_in, den_in, kvs, rest = refs[0], refs[1], refs[2], refs[3 : 3 + n_kv], refs[3 + n_kv :]
        if last:
            outs, (key_ref, val_ref) = rest[:-2], rest[-2:]
        else:
            num_ref, den_ref, key_ref, val_ref = rest

    for j, kv_ref in enumerate(kvs):
        rows = pl.ds(j * PAIR, PAIR)
        for h in range(3):
            key_ref[rows, pl.ds(h * 256, HD)] = kv_ref[:PAIR, pl.ds(h * HD, HD)]
        val_ref[rows, :] = kv_ref[:PAIR, WIDE:]

        def put(i, block):
            at = pl.ds(j * PAIR + i * ROWS, ROWS)
            for h in range(3):
                key_ref[at, pl.ds(h * 256 + HD, HD)] = block

        lanes_to_rows(kv_ref, put, lambda level, here: jnp.where(level == here, 1.0, 0.0))

    scale = HD**-0.5 * math.log2(math.e)
    rows = pl.ds(row0, nrows)
    dens = []
    for h in range(3):
        cols = pl.ds(h * HD, HD)
        wide = pl.ds(h * 256, 256)
        scores = lax.dot_general(
            qx_ref[rows, wide], key_ref[:, wide], (((1,), (1,)), ((), ())),
            preferred_element_type=F32,
        )
        weights = jnp.exp2(scores * scale)
        den = jnp.sum(weights, axis=1, keepdims=True)
        num = jnp.dot(weights.astype(BF16), val_ref[:, cols], preferred_element_type=F32)
        if not first:
            num = num + num_in[rows, cols]
            den = den + den_in[rows, h : h + 1]
        if last:
            done = (num / den).astype(BF16)
            for i, out_ref in enumerate(outs):
                out_ref[:, cols] = done[i * ROWS : (i + 1) * ROWS]
        else:
            num_ref[:, cols] = num
            dens.append(den)
    if not last:
        lane = lax.broadcasted_iota(jnp.int32, (QROWS, HD), 1)
        den_ref[...] = jnp.where(lane == 0, dens[0], jnp.where(lane == 1, dens[1], dens[2]))


def attend(kvs, queries=None, state=None, last=None, after=()):
    n_kv = len(kvs)
    first = state is None
    row0, nrows = (0, QROWS) if last is None else last
    args = (list(queries) if first else list(state)) + list(kvs)
    if last is None:
        outs = [shaped(QROWS, WIDE), shaped(QROWS, HD)]
        if first:
            outs.append(shaped(QROWS, 768, kind=BF16))
    else:
        outs = [shaped(ROWS, WIDE, kind=BF16)] * (nrows // ROWS)
    got = call(
        functools.partial(attend_kernel, len(after), n_kv, first, last is not None, row0, nrows),
        list(after) + args,
        [ANY] * len(after) + [VM] * len(args),
        outs,
        (4 * nrows * PAIR * n_kv * WIDE * 2, 2000000, nrows * PAIR * 3 * n_kv),
        [
            pltpu.VMEM((n_kv * PAIR, 768), BF16),
            pltpu.VMEM((n_kv * PAIR, WIDE), BF16),
        ],
    )
    if last is not None:
        return got
    return (got[2] if first else state[0], got[0], got[1])


def out_rows(where_ref, step):
    return pl.ds(pl.multiple_of(lax.rem(where_ref[0] + step, 4) * WIDE, 128), WIDE)


def out_first_kernel(where_ref, a_ref, w_ref, part_ref):
    part_ref[...] = jnp.dot(a_ref[...], w_ref[out_rows(where_ref, 0), :], preferred_element_type=F32)


def out_first(where, piece, out_weight):
    return call(
        out_first_kernel,
        (where, piece, out_weight),
        [SM, VM, VM],
        [shaped(ROWS, D)],
        (2 * ROWS * WIDE * D, 5000000, 0),
    )[0]


def out_rest_kernel(own, where_ref, after_ref, part_ref, a1, a2, a3, w_ref, gate_ref, term_ref):
    core = where_ref[1]
    half = core if own else 1 - core
    cols = pl.ds(pl.multiple_of(half * HALF, 128), HALF)
    branch = part_ref[:, cols]
    for piece, step in ((a1, 1), (a2, 3), (a3, 2)):
        weight = w_ref[out_rows(where_ref, step), cols]
        branch = branch + jnp.dot(piece[...], weight, preferred_element_type=F32)
    term_ref[...] = gate_ref[:, cols] * branch


def out_rest(own, where, after, part, pieces, out_weight, gate):
    return call(
        functools.partial(out_rest_kernel, own),
        (where, after, part, *pieces, out_weight, gate),
        [SM, ANY] + [VM] * 6,
        [shaped(ROWS, HALF)],
        (ROWS * 3 * WIDE * D, 5000000, 0),
    )[0]


def add_kernel(a_ref, b_ref, after_ref, out_ref, wire_ref):
    total = a_ref[...] + b_ref[...].astype(F32)
    out_ref[...] = total
    wire_ref[...] = total.astype(wire_ref.dtype)


def add_up(a, b, wire, after):
    return call(
        add_kernel,
        (a, b, after),
        [VM, VM, ANY],
        [shaped(ROWS, HALF), shaped(ROWS, HALF, kind=wire)],
        (ROWS * HALF, 2000000, 0),
    )


def before_sum(where_ref, got_ref, far_ref):
    chip = where_ref[2]
    near = jnp.where(lax.rem(chip, 2) == 1, got_ref[...].astype(F32), 0.0)
    return near + jnp.where(chip >= 2, far_ref[...].astype(F32), 0.0)


def back_kernel(where_ref, after_ref, keep_ref, got_ref, far_ref, out_ref):
    extra = jnp.where(where_ref[1] == 0, keep_ref[...], 0.0)
    out_ref[...] = before_sum(where_ref, got_ref, far_ref) + extra


def back_sum(where, after, keep, got, far):
    return call(
        back_kernel,
        (where, after, keep, got, far),
        [SM, ANY] + [VM] * 3,
        [shaped(ROWS, HALF)],
        (ROWS * HALF, 2000000, 0),
    )[0]


def join_kernel(where_ref, base_ref, keep_ref, give_ref, beside_ref, got_ref, far_ref, back_ref, out_ref):
    core = where_ref[1]
    mine = pl.ds(pl.multiple_of(core * HALF, 128), HALF)
    other = pl.ds(pl.multiple_of((1 - core) * HALF, 128), HALF)
    own = before_sum(where_ref, got_ref, far_ref) + jnp.where(core == 1, beside_ref[...], 0.0)
    out_ref[:, mine] = base_ref[:, mine] + (keep_ref[...] + own)
    out_ref[:, other] = base_ref[:, other] + (give_ref[...] + back_ref[...])


def join(where, base, keep, give, beside, got, far, back):
    return call(
        join_kernel,
        (where, base, keep, give, beside, got, far, back),
        [SM] + [VM] * 7,
        [shaped(ROWS, D)],
        (ROWS * D * 2, 4000000, 0),
    )[0]


SWAP = pairs(lambda x, c, y, z: (x, 1 - c, y, z))
ROUND1 = pairs(lambda x, c, y, z: (x ^ 1, c, y, z))
ROUND2 = pairs(lambda x, c, y, z: (3 - x, c, y, z) if x < 2 else None)


def held(x):
    return pltpu.with_memory_space_constraint(x, pltpu.HBM)


def per_device(iterate, anchor, frame_index, noise_steps, qkv_weight, out_weight, mod_weight):
    qkv_weight, mod_weight = held(qkv_weight), held(mod_weight)
    tm = lax.axis_index("tm")
    ctx = lax.axis_index("ctx")
    chip, core = tm // 2, tm % 2
    place = jnp.where(core == 0, ctx // 4, ctx % 4)
    where = jnp.stack([place, core, chip]).astype(jnp.int32)
    latent = held(iterate[0])
    features, gap = frame_features(noise_steps[0])
    gap = jnp.pad(gap, (0, 128 - NF))[None, :]
    frame_row = jnp.pad(frame_index, (0, 256 - ROWS))[None, :]

    tie = lax.optimization_barrier
    mine, latent = normed_pack(latent, frame_row, features, mod_weight)
    from_prev = send(mine, along("a", 1))
    from_next = send(mine, along("a", -1))
    lat_keep, lat_give = lat_terms(where, latent, frame_row, gap)
    lat_beside = send(lat_give, SWAP)
    gate, weight = side_terms(
        where, lat_give, frame_row, gap, features, mod_weight, qkv_weight
    )
    mine_later, weight = tie((mine, weight))
    from_far = send(mine_later, along("a", 2))
    lat_both, lat_wire = add_up(lat_keep, lat_beside, F32, weight)
    lat_got = send(lat_wire, ROUND1)

    q0, kv0 = project(mine, from_prev, weight, after=(lat_wire,))
    up0 = send(kv0, along("b", 1))
    down0 = send(kv0, along("b", -1))
    q1, kv1 = project(from_next, from_far, weight, after=(kv0,))
    down1 = send(kv1, along("b", -1))
    up1 = send(kv1, along("b", 1))
    far0 = send(up0, along("b", 1))
    state = attend([kv0, kv1], queries=(q0, q1))
    state = attend([up0, down0], state=state)
    down1_later, _ = tie((down1, state[1]))
    far1 = send(down1_later, along("b", -1))
    _, lat_wire = add_up(lat_both, lat_got, F32, state[1])
    lat_far = send(lat_wire, ROUND2)
    state = attend([up1, down1], state=state, after=(lat_wire,))
    a1, a2, a3 = attend([far0, far1], state=state, last=(ROWS, 3 * ROWS))
    b3 = send(a3, along("a", -2))
    b1 = send(a1, along("a", -1))
    b2 = send(a2, along("a", 1))
    (a0,) = attend([far0, far1], state=state, last=(0, ROWS), after=(a1,))
    part = out_first(where, a0, out_weight)
    pieces = (b1, b2, b3)
    give = out_rest(False, where, part, part, pieces, out_weight, gate)
    beside = send(give, SWAP)
    keep = out_rest(True, where, give, part, pieces, out_weight, gate)
    both, wire = add_up(keep, beside, BF16, keep)
    got = send(wire, ROUND1)
    lat_sum = back_sum(where, wire, lat_keep, lat_got, lat_far)
    lat_back = send(lat_sum, SWAP)
    base = join(where, anchor, lat_keep, lat_give, lat_beside, lat_got, lat_far, lat_back)
    _, wire = add_up(both, got, BF16, base)
    far = send(wire, ROUND2)
    back = send(back_sum(where, far, keep, got, far), SWAP)
    return join(where, base, keep, give, beside, got, far, back)[None]


def solution(mesh):
    placed = (P("tm", "ctx", None), P("ctx", None), P("ctx"), P("tm", None), P(), P(), P())

    return jax.shard_map(
        per_device, mesh=mesh, in_specs=placed, out_specs=P("tm", "ctx", None), check_vma=False
    )
```

```python
import functools
import math

import jax
import jax.numpy as jnp
from jax import lax
from jax.experimental import pallas as pl
from jax.experimental.pallas import tpu as pltpu
from jax.sharding import PartitionSpec as P


HD = 128
NSCHED = 12
NF = 16
D = 1536
ROWS = 168
PACK = 176
WIDE = 384
PAIR = 2 * ROWS
PAIRPACK = PAIR + 8
QROWS = 4 * ROWS
HALF = D // 2
QUART = D // 4
BIG = 131072.0
AXES = ("tm", "ctx")

shift_factor = 5.0
norm_eps = 1e-06
F32 = jnp.float32
BF16 = jnp.bfloat16
VM = pl.BlockSpec(memory_space=pltpu.VMEM)
SM = pl.BlockSpec(memory_space=pltpu.SMEM)
ANY = pl.BlockSpec(memory_space=pl.ANY)
HBM = pl.BlockSpec(memory_space=pltpu.HBM)


def shaped(*shape, kind=F32):
    return jax.ShapeDtypeStruct(shape, kind)


def call(kernel, args, specs, outs, cost, scratch=(), mib=24, out_specs=None):
    flops, moved, exps = cost
    return run_kernel(kernel, args, specs, outs, flops, moved, exps, scratch, mib, out_specs)


def run_kernel(kernel, args, specs, outs, flops, moved, exps, scratch, mib, out_specs):
    return pl.pallas_call(
        kernel,
        in_specs=specs,
        out_specs=[VM] * len(outs) if out_specs is None else out_specs,
        out_shape=outs,
        scratch_shapes=list(scratch),
        compiler_params=pltpu.CompilerParams(vmem_limit_bytes=mib << 20),
        cost_estimate=pl.CostEstimate(flops=flops, bytes_accessed=moved, transcendentals=exps),
    )(*args)


def place_of(x, c, y, z):
    return ((x % 4) * 2 + c % 2) * 16 + (y % 4) * 4 + z % 4


def pairs(move):
    found = []
    for x in range(4):
        for c in range(2):
            for y in range(4):
                for z in range(4):
                    to = move(x, c, y, z)
                    if to is not None:
                        found.append((place_of(x, c, y, z), place_of(*to)))
    return found


def along(ring, step):
    def move(x, c, y, z):
        if (c == 0) == (ring == "a"):
            return (x, c, y + step, z)
        return (x, c, y, z + step)

    return pairs(move)


def send(value, route):
    return lax.ppermute(value, AXES, route)


def noise_level(level_index):
    fraction = level_index / NSCHED
    return shift_factor * fraction / (1.0 + (shift_factor - 1.0) * fraction)


def frame_features(steps_row):
    level_float = steps_row.astype(F32)
    upper = noise_level(level_float + 1.0)
    lower = noise_level(level_float)
    half_freq = 128
    rates = jnp.exp(-math.log(10000.0) * jnp.arange(half_freq, dtype=F32) / half_freq)
    angles = (1000.0 * upper)[:, None] * rates[None, :]
    features = jnp.concatenate([jnp.cos(angles), jnp.sin(angles)], axis=1).astype(BF16)
    return features, upper - lower


def split3(value):
    high = value.astype(BF16)
    rest = value - high.astype(F32)
    mid = rest.astype(BF16)
    low = (rest - mid.astype(F32)).astype(BF16)
    return jnp.concatenate([high, mid, low], axis=0)


def ones_by_frame(frame_row, rows):
    level = lax.broadcasted_iota(jnp.int32, (128, 256), 0)
    here = jnp.broadcast_to(frame_row, (128, 256))
    hit = jnp.where(jnp.logical_and(level % NF == here, level < rows), 1.0, 0.0)
    return hit.T[:ROWS]


def pick_rows(ones, table):
    return jnp.dot(ones[:, : 3 * NF], split3(table), preferred_element_type=F32)


def norm_kernel(latent_hbm, frame_ref, feat_ref, mod_hbm, out_ref, lat_ref, mod_ref, picked_ref, sems):
    copies = [
        pltpu.make_async_copy(mod_hbm.at[:, pl.ds(i * D, D)], mod_ref.at[i], sems.at[i])
        for i in range(2)
    ]
    copies.append(pltpu.make_async_copy(latent_hbm, lat_ref, sems.at[2]))
    for one in copies:
        one.start()
    ones = ones_by_frame(frame_ref[...], 3 * NF).astype(BF16)
    for half in range(2):
        copies[half].wait()
        table = jnp.dot(feat_ref[...], mod_ref[half], preferred_element_type=F32)
        picked_ref[:, pl.ds(half * D, D)] = pick_rows(ones, table)
    copies[2].wait()

    def block(i, carry):
        rows = pl.ds(pl.multiple_of(i * 24, 8), 24)
        latent = lat_ref[rows, :]
        center = latent - jnp.mean(latent, axis=-1, keepdims=True)
        spread = jnp.mean(center * center, axis=-1, keepdims=True)
        normal = center * lax.rsqrt(spread + norm_eps)
        out = normal * (1.0 + picked_ref[rows, D:]) + picked_ref[rows, :D]
        out_ref[rows, :] = out.astype(BF16)
        return carry

    lax.fori_loop(0, ROWS // 24, block, 0)
    out_ref[ROWS:, :] = jnp.zeros((PACK - ROWS, D), BF16)
    out_ref[ROWS:, :256] = jnp.broadcast_to(frame_ref[...], (8, 256)).astype(F32).astype(BF16)


def normed_pack(latent, frame_row, features, mod_weight):
    return call(
        norm_kernel,
        (latent, frame_row, features, mod_weight),
        [HBM, VM, VM, HBM],
        [shaped(PACK, D, kind=BF16), shaped(ROWS, D)],
        (30000000, 4000000, 0),
        [
            pltpu.VMEM((2, 256, D), BF16),
            pltpu.VMEM((ROWS, 2 * D), F32),
            pltpu.SemaphoreType.DMA((3,)),
        ],
    )


def frame_gap(ones, gap_ref):
    return jnp.sum(ones[:, :NF] * gap_ref[:, :NF], axis=1, keepdims=True)


def lat_kernel(where_ref, latent_ref, frame_ref, gap_ref, keep_ref, give_ref):
    core = where_ref[1]
    gap = frame_gap(ones_by_frame(frame_ref[...], NF), gap_ref)
    mine = pl.ds(pl.multiple_of(core * HALF, 128), HALF)
    other = pl.ds(pl.multiple_of((1 - core) * HALF, 128), HALF)
    keep_ref[...] = -gap * latent_ref[:, mine]
    give_ref[...] = -gap * latent_ref[:, other]


def lat_terms(where, latent, frame_row, gap):
    return call(
        lat_kernel,
        (where, latent, frame_row, gap),
        [SM, VM, VM, VM],
        [shaped(ROWS, HALF), shaped(ROWS, HALF)],
        (ROWS * D, 2000000, 0),
    )


def side_kernel(
    where_ref, after_ref, frame_ref, gap_ref, feat_ref, mod_hbm, qkv_hbm, gate_ref, w_ref, mod_ref, sems
):
    place = where_ref[0]
    copies = [pltpu.make_async_copy(mod_hbm.at[:, pl.ds(2 * D, D)], mod_ref, sems.at[0])]
    for i in range(3):
        cols = pl.ds(pl.multiple_of(i * D + place * WIDE, 128), WIDE)
        copies.append(
            pltpu.make_async_copy(
                qkv_hbm.at[:, cols], w_ref.at[:, pl.ds(i * WIDE, WIDE)], sems.at[1 + i]
            )
        )
    for one in copies:
        one.start()
    ones = ones_by_frame(frame_ref[...], 3 * NF)
    gap = frame_gap(ones, gap_ref)
    copies[0].wait()
    table = jnp.dot(feat_ref[...], mod_ref[...], preferred_element_type=F32)
    gate_ref[...] = -gap * pick_rows(ones.astype(BF16), table)
    for one in copies[1:]:
        one.wait()


def side_terms(where, after, frame_row, gap, features, mod_weight, qkv_weight):
    return call(
        side_kernel,
        (where, after, frame_row, gap, features, mod_weight, qkv_weight),
        [SM, ANY, VM, VM, VM, HBM, HBM],
        [shaped(ROWS, D), shaped(D, 3 * WIDE, kind=BF16)],
        (30000000, 6000000, 0),
        [pltpu.VMEM((256, D), BF16), pltpu.SemaphoreType.DMA((4,))],
    )


def head_normed(one):
    mean = jnp.mean(one * one, axis=-1, keepdims=True)
    return (one * lax.rsqrt(mean + norm_eps)).astype(BF16)


def qkv_kernel(n_after, *refs):
    n0, n1, w_ref, q_ref, kv_ref, tok_ref = refs[n_after:]
    tok_ref[:ROWS, :] = n0[:ROWS, :]
    tok_ref[ROWS:, :] = n1[:ROWS, :]
    tokens = tok_ref[...]
    for h in range(3):
        cols = pl.ds(h * WIDE, WIDE)
        got = jnp.dot(tokens, w_ref[:, cols], preferred_element_type=F32)
        if h == 2:
            kv_ref[:PAIR, WIDE:] = got.astype(BF16)
            continue
        target = q_ref if h == 0 else kv_ref
        for i in range(3):
            part = pl.ds(i * HD, HD)
            target[:PAIR, part] = head_normed(got[:, i * HD : (i + 1) * HD])
    kv_ref[PAIR:, :256] = n0[ROWS:, :256]
    kv_ref[PAIR:, 256:512] = n1[ROWS:, :256]
    kv_ref[PAIR:, 512:] = jnp.zeros((8, 256), BF16)


def project(n0, n1, weight, after=()):
    return call(
        functools.partial(qkv_kernel, len(after)),
        (*after, n0, n1, weight),
        [ANY] * len(after) + [VM] * 3,
        [shaped(PAIR, WIDE, kind=BF16), shaped(PAIRPACK, 2 * WIDE, kind=BF16)],
        (2 * PAIR * D * 3 * WIDE, 5000000, 0),
        [pltpu.VMEM((PAIR, D), BF16)],
    )


def lanes_to_rows(pack_ref, put, make):
    for i in range(2):
        here = pack_ref[PAIR : PAIR + 1, i * 256 : (i + 1) * 256].astype(F32)
        level = lax.broadcasted_iota(jnp.int32, (HD, 256), 0).astype(F32)
        put(i, make(level, here).T[:ROWS].astype(BF16))


def attend_kernel(n_after, n_kv, first, last, row0, nrows, *refs):
    refs = list(refs)[n_after:]
    if first:
        q0, q1, kvs, rest = refs[0], refs[1], refs[2 : 2 + n_kv], refs[2 + n_kv :]
        num_ref, den_ref, qx_ref, key_ref, val_ref = rest
        for j, (q_ref, kv_ref) in enumerate(((q0, kvs[0]), (q1, kvs[1]))):
            rows = pl.ds(j * PAIR, PAIR)
            for h in range(3):
                qx_ref[rows, pl.ds(h * 256, HD)] = q_ref[:, pl.ds(h * HD, HD)]

            def put(i, block):
                at = pl.ds(j * PAIR + i * ROWS, ROWS)
                for h in range(3):
                    qx_ref[at, pl.ds(h * 256 + HD, HD)] = block

            lanes_to_rows(kv_ref, put, lambda level, here: jnp.where(level > here, -BIG, 0.0))
    else:
        qx_ref, num_in, den_in, kvs, rest = refs[0], refs[1], refs[2], refs[3 : 3 + n_kv], refs[3 + n_kv :]
        if last:
            outs, (key_ref, val_ref) = rest[:-2], rest[-2:]
        else:
            num_ref, den_ref, key_ref, val_ref = rest

    for j, kv_ref in enumerate(kvs):
        rows = pl.ds(j * PAIR, PAIR)
        for h in range(3):
            key_ref[rows, pl.ds(h * 256, HD)] = kv_ref[:PAIR, pl.ds(h * HD, HD)]
        val_ref[rows, :] = kv_ref[:PAIR, WIDE:]

        def put(i, block):
            at = pl.ds(j * PAIR + i * ROWS, ROWS)
            for h in range(3):
                key_ref[at, pl.ds(h * 256 + HD, HD)] = block

        lanes_to_rows(kv_ref, put, lambda level, here: jnp.where(level == here, 1.0, 0.0))

    scale = HD**-0.5 * math.log2(math.e)
    rows = pl.ds(row0, nrows)
    dens = []
    for h in range(3):
        cols = pl.ds(h * HD, HD)
        wide = pl.ds(h * 256, 256)
        scores = lax.dot_general(
            qx_ref[rows, wide], key_ref[:, wide], (((1,), (1,)), ((), ())),
            preferred_element_type=F32,
        )
        weights = jnp.exp2(scores * scale)
        den = jnp.sum(weights, axis=1, keepdims=True)
        num = jnp.dot(weights.astype(BF16), val_ref[:, cols], preferred_element_type=F32)
        if not first:
            num = num + num_in[rows, cols]
            den = den + den_in[rows, h : h + 1]
        if last:
            done = (num / den).astype(BF16)
            for i, out_ref in enumerate(outs):
                out_ref[:, cols] = done[i * ROWS : (i + 1) * ROWS]
        else:
            num_ref[:, cols] = num
            dens.append(den)
    if not last:
        lane = lax.broadcasted_iota(jnp.int32, (QROWS, HD), 1)
        den_ref[...] = jnp.where(lane == 0, dens[0], jnp.where(lane == 1, dens[1], dens[2]))


def attend(kvs, queries=None, state=None, last=None, after=()):
    n_kv = len(kvs)
    first = state is None
    row0, nrows = (0, QROWS) if last is None else last
    args = (list(queries) if first else list(state)) + list(kvs)
    if last is None:
        outs = [shaped(QROWS, WIDE), shaped(QROWS, HD)]
        if first:
            outs.append(shaped(QROWS, 768, kind=BF16))
    else:
        outs = [shaped(ROWS, WIDE, kind=BF16)] * (nrows // ROWS)
    got = call(
        functools.partial(attend_kernel, len(after), n_kv, first, last is not None, row0, nrows),
        list(after) + args,
        [ANY] * len(after) + [VM] * len(args),
        outs,
        (4 * nrows * PAIR * n_kv * WIDE * 2, 2000000, nrows * PAIR * 3 * n_kv),
        [
            pltpu.VMEM((n_kv * PAIR, 768), BF16),
            pltpu.VMEM((n_kv * PAIR, WIDE), BF16),
        ],
    )
    if last is not None:
        return got
    return (got[2] if first else state[0], got[0], got[1])


def out_rows(where_ref, step):
    return pl.ds(pl.multiple_of(lax.rem(where_ref[0] + step, 4) * WIDE, 128), WIDE)


def out_first_kernel(where_ref, a_ref, w_ref, part_ref):
    part_ref[...] = jnp.dot(a_ref[...], w_ref[out_rows(where_ref, 0), :], preferred_element_type=F32)


def out_first(where, piece, out_weight):
    return call(
        out_first_kernel,
        (where, piece, out_weight),
        [SM, VM, VM],
        [shaped(ROWS, D)],
        (2 * ROWS * WIDE * D, 5000000, 0),
    )[0]


def out_rest_kernel(own, where_ref, after_ref, part_ref, a1, a2, a3, w_ref, gate_ref, term_ref):
    core = where_ref[1]
    half = core if own else 1 - core
    cols = pl.ds(pl.multiple_of(half * HALF, 128), HALF)
    branch = part_ref[:, cols]
    for piece, step in ((a1, 1), (a2, 3), (a3, 2)):
        weight = w_ref[out_rows(where_ref, step), cols]
        branch = branch + jnp.dot(piece[...], weight, preferred_element_type=F32)
    term_ref[...] = gate_ref[:, cols] * branch


def out_rest(own, where, after, part, pieces, out_weight, gate):
    return call(
        functools.partial(out_rest_kernel, own),
        (where, after, part, *pieces, out_weight, gate),
        [SM, ANY] + [VM] * 6,
        [shaped(ROWS, HALF)],
        (ROWS * 3 * WIDE * D, 5000000, 0),
    )[0]


def add_kernel(n_parts, a_ref, b_ref, after_ref, *outs):
    total = a_ref[...] + b_ref[...].astype(F32)
    if len(outs) > n_parts:
        outs[0][...] = total
    wide = total.shape[1] // n_parts
    for i, wire_ref in enumerate(outs[-n_parts:]):
        wire_ref[...] = total[:, i * wide : (i + 1) * wide].astype(wire_ref.dtype)


def add_up(a, b, wire, after, n_parts=1, keep=False):
    wide = a.shape[1]
    outs = [shaped(ROWS, wide // n_parts, kind=wire)] * n_parts
    return call(
        functools.partial(add_kernel, n_parts),
        (a, b, after),
        [VM, VM, ANY],
        ([shaped(ROWS, wide)] if keep else []) + outs,
        (ROWS * wide, 2000000, 0),
    )


def pair_kernel(part, both_ref, got_ref, after_ref, wire_ref):
    total = both_ref[:, pl.ds(part * QUART, QUART)] + got_ref[...].astype(F32)
    wire_ref[...] = total.astype(wire_ref.dtype)


def pair_up(part, both, got, after):
    return call(
        functools.partial(pair_kernel, part),
        (both, got, after),
        [VM, VM, ANY],
        [shaped(ROWS, QUART, kind=BF16)],
        (ROWS * QUART, 1000000, 0),
    )[0]


def before_sum(where_ref, got_ref, far_ref):
    chip = where_ref[2]
    near = jnp.where(lax.rem(chip, 2) == 1, got_ref[...].astype(F32), 0.0)
    return near + jnp.where(chip >= 2, far_ref[...].astype(F32), 0.0)


def back_kernel(col0, where_ref, after_ref, keep_ref, got_ref, far_ref, out_ref):
    mine = keep_ref[:, pl.ds(col0, got_ref.shape[1])]
    extra = jnp.where(where_ref[1] == 0, mine, 0.0)
    out_ref[...] = before_sum(where_ref, got_ref, far_ref) + extra


def back_sum(where, after, keep, got, far, col0=0):
    return call(
        functools.partial(back_kernel, col0),
        (where, after, keep, got, far),
        [SM, ANY] + [VM] * 3,
        [shaped(*got.shape)],
        (ROWS * HALF, 2000000, 0),
    )[0]


def base_kernel(where_ref, after_ref, anchor_ref, keep_ref, give_ref, beside_ref, got_ref, far_ref, back_ref, out_ref):
    core = where_ref[1]
    mine = pl.ds(pl.multiple_of(core * HALF, 128), HALF)
    other = pl.ds(pl.multiple_of((1 - core) * HALF, 128), HALF)
    own = before_sum(where_ref, got_ref, far_ref) + jnp.where(core == 1, beside_ref[...], 0.0)
    out_ref[:, mine] = anchor_ref[:, mine] + (keep_ref[...] + own)
    out_ref[:, other] = anchor_ref[:, other] + (give_ref[...] + back_ref[...])


def base_sum(where, after, *terms):
    return call(
        base_kernel,
        (where, after, *terms),
        [SM, ANY] + [VM] * 7,
        [shaped(ROWS, D)],
        (ROWS * D * 2, 4000000, 0),
    )[0]


def final_kernel(own, where_ref, *refs):
    core = where_ref[1]
    if own:
        _, base_ref, keep_ref, beside_ref, g0, g1, f0, f1, out_hbm, buf_ref, sems = refs
    else:
        _, base_ref, give_ref, b0, b1, out_hbm, buf_ref, sems = refs
    half = core if own else 1 - core
    copies = []
    for i in range(2):
        part = pl.ds(i * QUART, QUART)
        at = pl.ds(pl.multiple_of(half * HALF + i * QUART, 128), QUART)
        if own:
            got, far = ((g0, f0), (g1, f1))[i]
            more = before_sum(where_ref, got, far) + jnp.where(core == 1, beside_ref[:, part], 0.0)
            term = keep_ref[:, part] + more
        else:
            term = give_ref[:, part] + (b0, b1)[i][...]
        buf_ref[:, part] = base_ref[:, at] + term
        copies.append(pltpu.make_async_copy(buf_ref.at[:, part], out_hbm.at[:, at], sems.at[i]))
        copies[-1].start()
    for one in copies:
        one.wait()


def final_sum(own, args):
    n = len(args)
    return pl.pallas_call(
        functools.partial(final_kernel, own),
        in_specs=[SM, HBM if not own else ANY] + [VM] * (n - 2),
        out_specs=HBM,
        out_shape=shaped(ROWS, D),
        input_output_aliases={} if own else {1: 0},
        scratch_shapes=[pltpu.VMEM((ROWS, HALF), F32), pltpu.SemaphoreType.DMA((2,))],
        compiler_params=pltpu.CompilerParams(vmem_limit_bytes=24 << 20),
        cost_estimate=pl.CostEstimate(flops=ROWS * D, bytes_accessed=2000000, transcendentals=0),
        name="final_own" if own else "final_other",
    )(*args)


SWAP = pairs(lambda x, c, y, z: (x, 1 - c, y, z))
ROUND1 = pairs(lambda x, c, y, z: (x ^ 1, c, y, z))
ROUND2 = pairs(lambda x, c, y, z: (3 - x, c, y, z) if x < 2 else None)


def held(x):
    return pltpu.with_memory_space_constraint(x, pltpu.HBM)


def per_device(iterate, anchor, frame_index, noise_steps, qkv_weight, out_weight, mod_weight):
    qkv_weight, mod_weight = held(qkv_weight), held(mod_weight)
    tm = lax.axis_index("tm")
    ctx = lax.axis_index("ctx")
    chip, core = tm // 2, tm % 2
    place = jnp.where(core == 0, ctx // 4, ctx % 4)
    where = jnp.stack([place, core, chip]).astype(jnp.int32)
    latent = held(iterate[0])
    features, gap = frame_features(noise_steps[0])
    gap = jnp.pad(gap, (0, 128 - NF))[None, :]
    frame_row = jnp.pad(frame_index, (0, 256 - ROWS))[None, :]

    tie = lax.optimization_barrier
    mine, latent = normed_pack(latent, frame_row, features, mod_weight)
    from_prev = send(mine, along("a", 1))
    from_next = send(mine, along("a", -1))
    from_far = send(mine, along("a", 2))
    lat_keep, lat_give = lat_terms(where, latent, frame_row, gap)
    lat_beside = send(lat_give, SWAP)
    gate, weight = side_terms(
        where, lat_give, frame_row, gap, features, mod_weight, qkv_weight
    )
    (lat_both,) = add_up(lat_keep, lat_beside, F32, weight)
    lat_got = send(lat_both, ROUND1)

    q0, kv0 = project(mine, from_prev, weight, after=(lat_both,))
    up0 = send(kv0, along("b", 1))
    down0 = send(kv0, along("b", -1))
    q1, kv1 = project(from_next, from_far, weight, after=(kv0,))
    down1 = send(kv1, along("b", -1))
    up1 = send(kv1, along("b", 1))
    far0 = send(up0, along("b", 1))
    state = attend([kv0, kv1], queries=(q0, q1))
    state = attend([up0, down0], state=state)
    down1_later, _ = tie((down1, state[1]))
    far1 = send(down1_later, along("b", -1))
    (lat_wire,) = add_up(lat_both, lat_got, F32, state[1])
    lat_far = send(lat_wire, ROUND2)
    state = attend([up1, down1], state=state, after=(lat_wire,))
    a1, a2, a3 = attend([far0, far1], state=state, last=(ROWS, 3 * ROWS))
    b3 = send(a3, along("a", -2))
    b1 = send(a1, along("a", -1))
    b2 = send(a2, along("a", 1))
    (a0,) = attend([far0, far1], state=state, last=(0, ROWS), after=(a1,))
    part = out_first(where, a0, out_weight)
    pieces = (b1, b2, b3)
    give = out_rest(False, where, part, part, pieces, out_weight, gate)
    beside = send(give, SWAP)
    keep = out_rest(True, where, give, part, pieces, out_weight, gate)
    both, wire0, wire1 = add_up(keep, beside, BF16, keep, n_parts=2, keep=True)
    got0 = send(wire0, ROUND1)
    got1 = send(wire1, ROUND1)
    lat_sum = back_sum(where, wire0, lat_keep, lat_got, lat_far)
    lat_back = send(lat_sum, SWAP)
    pair0 = pair_up(0, both, got0, lat_sum)
    far0 = send(pair0, ROUND2)
    pair1 = pair_up(1, both, got1, pair0)
    far1 = send(pair1, ROUND2)
    base = base_sum(
        where, pair1, anchor, lat_keep, lat_give, lat_beside, lat_got, lat_far, lat_back
    )
    sum0 = back_sum(where, base, keep, got0, far0)
    back0 = send(sum0, SWAP)
    sum1 = back_sum(where, sum0, keep, got1, far1, QUART)
    back1 = send(sum1, SWAP)
    out = final_sum(True, (where, sum1, base, keep, beside, got0, got1, far0, far1))
    out = final_sum(False, (where, out, base, give, back0, back1))
    return out[None]


def solution(mesh):
    placed = (P("tm", "ctx", None), P("ctx", None), P("ctx"), P("tm", None), P(), P(), P())

    return jax.shard_map(
        per_device, mesh=mesh, in_specs=placed, out_specs=P("tm", "ctx", None), check_vma=False
    )
```

```python
import functools
import math

import jax
import jax.numpy as jnp
from jax import lax
from jax.experimental import pallas as pl
from jax.experimental.pallas import tpu as pltpu
from jax.sharding import PartitionSpec as P


HD = 128
NSCHED = 12
NF = 16
D = 1536
ROWS = 168
PACK = 176
WIDE = 384
PAIR = 2 * ROWS
PAIRPACK = PAIR + 8
QROWS = 4 * ROWS
HALF = D // 2
QUART = D // 4
BIG = 131072.0
AXES = ("tm", "ctx")

shift_factor = 5.0
norm_eps = 1e-06
F32 = jnp.float32
BF16 = jnp.bfloat16
VM = pl.BlockSpec(memory_space=pltpu.VMEM)
SM = pl.BlockSpec(memory_space=pltpu.SMEM)
ANY = pl.BlockSpec(memory_space=pl.ANY)
HBM = pl.BlockSpec(memory_space=pltpu.HBM)


def shaped(*shape, kind=F32):
    return jax.ShapeDtypeStruct(shape, kind)


def call(kernel, args, specs, outs, cost, scratch=(), mib=24, out_specs=None):
    flops, moved, exps = cost
    return run_kernel(kernel, args, specs, outs, flops, moved, exps, scratch, mib, out_specs)


def run_kernel(kernel, args, specs, outs, flops, moved, exps, scratch, mib, out_specs):
    return pl.pallas_call(
        kernel,
        in_specs=specs,
        out_specs=[VM] * len(outs) if out_specs is None else out_specs,
        out_shape=outs,
        scratch_shapes=list(scratch),
        compiler_params=pltpu.CompilerParams(vmem_limit_bytes=mib << 20),
        cost_estimate=pl.CostEstimate(flops=flops, bytes_accessed=moved, transcendentals=exps),
    )(*args)


def place_of(x, c, y, z):
    return ((x % 4) * 2 + c % 2) * 16 + (y % 4) * 4 + z % 4


def pairs(move):
    found = []
    for x in range(4):
        for c in range(2):
            for y in range(4):
                for z in range(4):
                    to = move(x, c, y, z)
                    if to is not None:
                        found.append((place_of(x, c, y, z), place_of(*to)))
    return found


def along(ring, step):
    def move(x, c, y, z):
        if (c == 0) == (ring == "a"):
            return (x, c, y + step, z)
        return (x, c, y, z + step)

    return pairs(move)


def send(value, route):
    return lax.ppermute(value, AXES, route)


def noise_level(level_index):
    fraction = level_index / NSCHED
    return shift_factor * fraction / (1.0 + (shift_factor - 1.0) * fraction)


def frame_features(steps_row):
    level_float = steps_row.astype(F32)
    upper = noise_level(level_float + 1.0)
    lower = noise_level(level_float)
    half_freq = 128
    rates = jnp.exp(-math.log(10000.0) * jnp.arange(half_freq, dtype=F32) / half_freq)
    angles = (1000.0 * upper)[:, None] * rates[None, :]
    features = jnp.concatenate([jnp.cos(angles), jnp.sin(angles)], axis=1).astype(BF16)
    return features, upper - lower


def split3(value):
    high = value.astype(BF16)
    rest = value - high.astype(F32)
    mid = rest.astype(BF16)
    low = (rest - mid.astype(F32)).astype(BF16)
    return jnp.concatenate([high, mid, low], axis=0)


def ones_by_frame(frame_row, rows):
    level = lax.broadcasted_iota(jnp.int32, (128, ROWS), 0)
    here = jnp.broadcast_to(frame_row, (128, ROWS))
    hit = jnp.where(jnp.logical_and(level % NF == here, level < rows), 1.0, 0.0)
    return hit.T


def pick_rows(ones, table):
    return jnp.dot(ones[:, : 3 * NF], split3(table), preferred_element_type=F32)


def norm_kernel(
    latent_hbm, frame_hbm, feat_ref, mod_hbm, out_ref, lat_ref, frame_ref, mod_ref, picked_ref, unit_ref, sems
):
    copies = [pltpu.make_async_copy(frame_hbm, frame_ref, sems.at[0])]
    for i in range(2):
        rows = pl.ds(i * (ROWS // 2 + 4), (88, 80)[i])
        copies.append(
            pltpu.make_async_copy(latent_hbm.at[rows, :], lat_ref.at[rows, :], sems.at[1 + i])
        )
    for i in range(4):
        cols = pl.ds(i * HALF, HALF)
        copies.append(pltpu.make_async_copy(mod_hbm.at[:, cols], mod_ref.at[:, cols], sems.at[3 + i]))
    for one in copies:
        one.start()
    copies[0].wait()
    ones = ones_by_frame(frame_ref[...], 3 * NF).astype(BF16)
    out_ref[ROWS:, :] = jnp.zeros((PACK - ROWS, D), BF16)
    out_ref[ROWS:, :ROWS] = jnp.broadcast_to(frame_ref[...], (8, ROWS)).astype(F32).astype(BF16)

    def normal(i, carry):
        rows = pl.ds(pl.multiple_of(i * 8, 8), 8)
        latent = lat_ref[rows, :]
        center = latent - jnp.mean(latent, axis=-1, keepdims=True)
        spread = jnp.mean(center * center, axis=-1, keepdims=True)
        unit_ref[rows, :] = center * lax.rsqrt(spread + norm_eps)
        return carry

    copies[1].wait()
    lax.fori_loop(0, 11, normal, 0, unroll=True)
    copies[2].wait()
    lax.fori_loop(11, 21, normal, 0, unroll=True)
    for i in range(4):
        cols = pl.ds(i * HALF, HALF)
        copies[3 + i].wait()
        table = jnp.dot(feat_ref[...], mod_ref[:, cols], preferred_element_type=F32)
        picked = pick_rows(ones, table)
        if i < 2:
            picked_ref[:, cols] = picked
        else:
            cols = pl.ds((i - 2) * HALF, HALF)
            out = unit_ref[:, cols] * (1.0 + picked) + picked_ref[:, cols]
            out_ref[:ROWS, cols] = out.astype(BF16)


def normed_pack(latent, frame_row, features, mod_weight):
    return call(
        norm_kernel,
        (latent, frame_row, features, mod_weight),
        [HBM, HBM, VM, HBM],
        [shaped(PACK, D, kind=BF16), shaped(ROWS, D), shaped(1, ROWS, kind=jnp.int32)],
        (30000000, 4000000, 0),
        [
            pltpu.VMEM((256, 2 * D), BF16),
            pltpu.VMEM((ROWS, D), F32),
            pltpu.VMEM((ROWS, D), F32),
            pltpu.SemaphoreType.DMA((7,)),
        ],
    )


def frame_gap(ones, gap_ref):
    return jnp.sum(ones[:, :NF] * gap_ref[:, :NF], axis=1, keepdims=True)


def lat_kernel(where_ref, latent_ref, frame_ref, gap_ref, keep_ref, give_ref):
    core = where_ref[1]
    gap = frame_gap(ones_by_frame(frame_ref[...], NF), gap_ref)
    mine = pl.ds(pl.multiple_of(core * HALF, 128), HALF)
    other = pl.ds(pl.multiple_of((1 - core) * HALF, 128), HALF)
    keep_ref[...] = -gap * latent_ref[:, mine]
    give_ref[...] = -gap * latent_ref[:, other]


def lat_terms(where, latent, frame_row, gap):
    return call(
        lat_kernel,
        (where, latent, frame_row, gap),
        [SM, VM, VM, VM],
        [shaped(ROWS, HALF), shaped(ROWS, HALF)],
        (ROWS * D, 2000000, 0),
    )


def side_kernel(
    where_ref, after_ref, frame_ref, gap_ref, feat_ref, mod_hbm, qkv_hbm, gate_ref, w_ref, mod_ref, sems
):
    place = where_ref[0]
    copies = [pltpu.make_async_copy(mod_hbm.at[:, pl.ds(2 * D, D)], mod_ref, sems.at[0])]
    for i in range(3):
        cols = pl.ds(pl.multiple_of(i * D + place * WIDE, 128), WIDE)
        copies.append(
            pltpu.make_async_copy(
                qkv_hbm.at[:, cols], w_ref.at[:, pl.ds(i * WIDE, WIDE)], sems.at[1 + i]
            )
        )
    for one in copies:
        one.start()
    ones = ones_by_frame(frame_ref[...], 3 * NF)
    gap = frame_gap(ones, gap_ref)
    copies[0].wait()
    table = jnp.dot(feat_ref[...], mod_ref[...], preferred_element_type=F32)
    gate_ref[...] = -gap * pick_rows(ones.astype(BF16), table)
    for one in copies[1:]:
        one.wait()


def side_terms(where, after, frame_row, gap, features, mod_weight, qkv_weight):
    return call(
        side_kernel,
        (where, after, frame_row, gap, features, mod_weight, qkv_weight),
        [SM, ANY, VM, VM, VM, HBM, HBM],
        [shaped(ROWS, D), shaped(D, 3 * WIDE, kind=BF16)],
        (30000000, 6000000, 0),
        [pltpu.VMEM((256, D), BF16), pltpu.SemaphoreType.DMA((4,))],
    )


def head_normed(one):
    mean = jnp.mean(one * one, axis=-1, keepdims=True)
    return (one * lax.rsqrt(mean + norm_eps)).astype(BF16)


def qkv_kernel(n_after, *refs):
    n0, n1, w_ref, q_ref, kv_ref, tok_ref = refs[n_after:]
    tok_ref[:ROWS, :] = n0[:ROWS, :]
    tok_ref[ROWS:, :] = n1[:ROWS, :]
    tokens = tok_ref[...]
    for h in range(3):
        cols = pl.ds(h * WIDE, WIDE)
        got = jnp.dot(tokens, w_ref[:, cols], preferred_element_type=F32)
        if h == 2:
            kv_ref[:PAIR, WIDE:] = got.astype(BF16)
            continue
        target = q_ref if h == 0 else kv_ref
        for i in range(3):
            part = pl.ds(i * HD, HD)
            target[:PAIR, part] = head_normed(got[:, i * HD : (i + 1) * HD])
    kv_ref[PAIR:, :256] = n0[ROWS:, :256]
    kv_ref[PAIR:, 256:512] = n1[ROWS:, :256]
    kv_ref[PAIR:, 512:] = jnp.zeros((8, 256), BF16)


def project(n0, n1, weight, after=()):
    return call(
        functools.partial(qkv_kernel, len(after)),
        (*after, n0, n1, weight),
        [ANY] * len(after) + [VM] * 3,
        [shaped(PAIR, WIDE, kind=BF16), shaped(PAIRPACK, 2 * WIDE, kind=BF16)],
        (2 * PAIR * D * 3 * WIDE, 5000000, 0),
        [pltpu.VMEM((PAIR, D), BF16)],
    )


def lanes_to_rows(pack_ref, put, make):
    for i in range(2):
        here = pack_ref[PAIR : PAIR + 1, i * 256 : (i + 1) * 256].astype(F32)
        level = lax.broadcasted_iota(jnp.int32, (HD, 256), 0).astype(F32)
        put(i, make(level, here).T[:ROWS].astype(BF16))


def attend_kernel(n_after, n_kv, first, last, row0, nrows, *refs):
    refs = list(refs)[n_after:]
    if first:
        q0, q1, kvs, rest = refs[0], refs[1], refs[2 : 2 + n_kv], refs[2 + n_kv :]
        num_ref, den_ref, qx_ref, key_ref, val_ref = rest
        for j, (q_ref, kv_ref) in enumerate(((q0, kvs[0]), (q1, kvs[1]))):
            rows = pl.ds(j * PAIR, PAIR)
            for h in range(3):
                qx_ref[rows, pl.ds(h * 256, HD)] = q_ref[:, pl.ds(h * HD, HD)]

            def put(i, block):
                at = pl.ds(j * PAIR + i * ROWS, ROWS)
                for h in range(3):
                    qx_ref[at, pl.ds(h * 256 + HD, HD)] = block

            lanes_to_rows(kv_ref, put, lambda level, here: jnp.where(level > here, -BIG, 0.0))
    else:
        qx_ref, num_in, den_in, kvs, rest = refs[0], refs[1], refs[2], refs[3 : 3 + n_kv], refs[3 + n_kv :]
        if last:
            outs, (key_ref, val_ref) = rest[:-2], rest[-2:]
        else:
            num_ref, den_ref, key_ref, val_ref = rest

    for j, kv_ref in enumerate(kvs):
        rows = pl.ds(j * PAIR, PAIR)
        for h in range(3):
            key_ref[rows, pl.ds(h * 256, HD)] = kv_ref[:PAIR, pl.ds(h * HD, HD)]
        val_ref[rows, :] = kv_ref[:PAIR, WIDE:]

        def put(i, block):
            at = pl.ds(j * PAIR + i * ROWS, ROWS)
            for h in range(3):
                key_ref[at, pl.ds(h * 256 + HD, HD)] = block

        lanes_to_rows(kv_ref, put, lambda level, here: jnp.where(level == here, 1.0, 0.0))
    used, whole_keys = n_kv * PAIR, key_ref.shape[0]
    extra = pl.ds(used, whole_keys - used)
    column = lax.broadcasted_iota(jnp.int32, (whole_keys - used, HD), 1)
    last_frame = jnp.where(column == NF, 1.0, 0.0).astype(BF16)
    for h in range(3):
        key_ref[extra, pl.ds(h * 256, HD)] = jnp.zeros((whole_keys - used, HD), BF16)
        key_ref[extra, pl.ds(h * 256 + HD, HD)] = last_frame
    val_ref[extra, :] = jnp.zeros((whole_keys - used, WIDE), BF16)

    scale = HD**-0.5 * math.log2(math.e)
    rows = pl.ds(row0, nrows)
    for h in range(3):
        cols = pl.ds(h * HD, HD)
        wide = pl.ds(h * 256, 256)
        scores = lax.dot_general(
            qx_ref[rows, wide], key_ref[:, wide], (((1,), (1,)), ((), ())),
            preferred_element_type=F32,
        )
        weights = jnp.exp2(scores * scale)
        den = weights[:, :HD]
        for i in range(1, whole_keys // HD):
            den = den + weights[:, i * HD : (i + 1) * HD]
        num = jnp.dot(weights.astype(BF16), val_ref[:, cols], preferred_element_type=F32)
        if not first:
            num = num + num_in[rows, cols]
            den = den + den_in[rows, cols]
        if last:
            done = (num / jnp.sum(den, axis=1, keepdims=True)).astype(BF16)
            for i, out_ref in enumerate(outs):
                out_ref[:, cols] = done[i * ROWS : (i + 1) * ROWS]
        else:
            num_ref[:, cols] = num
            den_ref[:, cols] = den


def attend(kvs, queries=None, state=None, last=None, after=()):
    n_kv = len(kvs)
    first = state is None
    row0, nrows = (0, QROWS) if last is None else last
    args = (list(queries) if first else list(state)) + list(kvs)
    if last is None:
        outs = [shaped(QROWS, WIDE), shaped(QROWS, WIDE)]
        if first:
            outs.append(shaped(QROWS, 768, kind=BF16))
    else:
        outs = [shaped(ROWS, WIDE, kind=BF16)] * (nrows // ROWS)
    got = call(
        functools.partial(attend_kernel, len(after), n_kv, first, last is not None, row0, nrows),
        list(after) + args,
        [ANY] * len(after) + [VM] * len(args),
        outs,
        (4 * nrows * PAIR * n_kv * WIDE * 2, 2000000, nrows * PAIR * 3 * n_kv),
        [
            pltpu.VMEM((-(-n_kv * PAIR // HD) * HD, 768), BF16),
            pltpu.VMEM((-(-n_kv * PAIR // HD) * HD, WIDE), BF16),
        ],
    )
    if last is not None:
        return got
    return (got[2] if first else state[0], got[0], got[1])


def out_rows(where_ref, step):
    return pl.ds(pl.multiple_of(lax.rem(where_ref[0] + step, 4) * WIDE, 128), WIDE)


def out_first_kernel(where_ref, a_ref, w_ref, part_ref):
    part_ref[...] = jnp.dot(a_ref[...], w_ref[out_rows(where_ref, 0), :], preferred_element_type=F32)


def out_first(where, piece, out_weight):
    return call(
        out_first_kernel,
        (where, piece, out_weight),
        [SM, VM, VM],
        [shaped(ROWS, D)],
        (2 * ROWS * WIDE * D, 5000000, 0),
    )[0]


def out_rest_kernel(own, where_ref, after_ref, part_ref, a1, a2, a3, w_ref, gate_ref, term_ref):
    core = where_ref[1]
    half = core if own else 1 - core
    cols = pl.ds(pl.multiple_of(half * HALF, 128), HALF)
    branch = part_ref[:, cols]
    for piece, step in ((a1, 1), (a2, 3), (a3, 2)):
        weight = w_ref[out_rows(where_ref, step), cols]
        branch = branch + jnp.dot(piece[...], weight, preferred_element_type=F32)
    term_ref[...] = gate_ref[:, cols] * branch


def out_rest(own, where, after, part, pieces, out_weight, gate):
    return call(
        functools.partial(out_rest_kernel, own),
        (where, after, part, *pieces, out_weight, gate),
        [SM, ANY] + [VM] * 6,
        [shaped(ROWS, HALF)],
        (ROWS * 3 * WIDE * D, 5000000, 0),
    )[0]


def add_kernel(n_parts, a_ref, b_ref, after_ref, *outs):
    total = a_ref[...] + b_ref[...].astype(F32)
    if len(outs) > n_parts:
        outs[0][...] = total
    wide = total.shape[1] // n_parts
    for i, wire_ref in enumerate(outs[-n_parts:]):
        wire_ref[...] = total[:, i * wide : (i + 1) * wide].astype(wire_ref.dtype)


def add_up(a, b, wire, after, n_parts=1, keep=False):
    wide = a.shape[1]
    outs = [shaped(ROWS, wide // n_parts, kind=wire)] * n_parts
    return call(
        functools.partial(add_kernel, n_parts),
        (a, b, after),
        [VM, VM, ANY],
        ([shaped(ROWS, wide)] if keep else []) + outs,
        (ROWS * wide, 2000000, 0),
    )


def pair_kernel(part, both_ref, got_ref, after_ref, wire_ref):
    total = both_ref[:, pl.ds(part * QUART, QUART)] + got_ref[...].astype(F32)
    wire_ref[...] = total.astype(wire_ref.dtype)


def pair_up(part, both, got, after):
    return call(
        functools.partial(pair_kernel, part),
        (both, got, after),
        [VM, VM, ANY],
        [shaped(ROWS, QUART, kind=BF16)],
        (ROWS * QUART, 1000000, 0),
    )[0]


def before_sum(where_ref, got_ref, far_ref):
    chip = where_ref[2]
    near = jnp.where(lax.rem(chip, 2) == 1, got_ref[...].astype(F32), 0.0)
    return near + jnp.where(chip >= 2, far_ref[...].astype(F32), 0.0)


def back_kernel(col0, where_ref, keep_ref, got_ref, far_ref, lat_ref, out_ref):
    cols = pl.ds(col0, got_ref.shape[1])
    extra = jnp.where(where_ref[1] == 0, keep_ref[:, cols], 0.0) + lat_ref[:, cols]
    out_ref[...] = before_sum(where_ref, got_ref, far_ref) + extra


def back_sum(where, after, keep, got, far, lat, col0=0):
    return call(
        lambda _, *refs: back_kernel(col0, *refs),
        (after, where, keep, got, far, lat),
        [ANY, SM] + [VM] * 4,
        [shaped(*got.shape)],
        (ROWS * HALF, 2000000, 0),
    )[0]


def base_kernel(
    where_ref, after_ref, anchor_ref, keep_ref, give_ref, beside_ref, got_ref, far_ref, own_ref, other_ref, back_ref
):
    core = where_ref[1]
    mine = pl.ds(pl.multiple_of(core * HALF, 128), HALF)
    other = pl.ds(pl.multiple_of((1 - core) * HALF, 128), HALF)
    before = before_sum(where_ref, got_ref, far_ref)
    own = before + jnp.where(core == 1, beside_ref[...], 0.0)
    own_ref[...] = anchor_ref[:, mine] + (keep_ref[...] + own)
    other_ref[...] = anchor_ref[:, other] + give_ref[...]
    back_ref[...] = before + jnp.where(core == 0, keep_ref[...], 0.0)


def base_sum(where, after, *terms):
    return call(
        base_kernel,
        (where, after, *terms),
        [SM, ANY] + [VM] * 6,
        [shaped(ROWS, HALF)] * 3,
        (ROWS * D * 2, 4000000, 0),
    )


def final_kernel(own, where_ref, *refs):
    core = where_ref[1]
    if own:
        _, base_ref, keep_ref, beside_ref, g0, g1, f0, f1, out_hbm, buf_ref, sems = refs
    else:
        _, base_ref, give_ref, b0, b1, out_hbm, buf_ref, sems = refs
    half = core if own else 1 - core
    copies = []
    for i in range(2):
        part = pl.ds(i * QUART, QUART)
        at = pl.ds(pl.multiple_of(half * HALF + i * QUART, 128), QUART)
        if own:
            got, far = ((g0, f0), (g1, f1))[i]
            more = before_sum(where_ref, got, far) + jnp.where(core == 1, beside_ref[:, part], 0.0)
            term = keep_ref[:, part] + more
        else:
            term = give_ref[:, part] + (b0, b1)[i][...]
        buf_ref[:, part] = base_ref[:, part] + term
        copies.append(pltpu.make_async_copy(buf_ref.at[:, part], out_hbm.at[:, at], sems.at[i]))
        copies[-1].start()
    for one in copies:
        one.wait()


def final_sum(own, args):
    n = len(args)
    return pl.pallas_call(
        functools.partial(final_kernel, own),
        in_specs=[SM, HBM if not own else ANY] + [VM] * (n - 2),
        out_specs=HBM,
        out_shape=shaped(ROWS, D),
        input_output_aliases={} if own else {1: 0},
        scratch_shapes=[pltpu.VMEM((ROWS, HALF), F32), pltpu.SemaphoreType.DMA((2,))],
        compiler_params=pltpu.CompilerParams(vmem_limit_bytes=24 << 20),
        cost_estimate=pl.CostEstimate(flops=ROWS * D, bytes_accessed=2000000, transcendentals=0),
        name="final_own" if own else "final_other",
    )(*args)


SWAP = pairs(lambda x, c, y, z: (x, 1 - c, y, z))
ROUND1 = pairs(lambda x, c, y, z: (x ^ 1, c, y, z))
ROUND2 = pairs(lambda x, c, y, z: (3 - x, c, y, z) if x < 2 else None)


def held(x):
    return pltpu.with_memory_space_constraint(x, pltpu.HBM)


def per_device(iterate, anchor, frame_index, noise_steps, qkv_weight, out_weight, mod_weight):
    qkv_weight, mod_weight = held(qkv_weight), held(mod_weight)
    tm = lax.axis_index("tm")
    ctx = lax.axis_index("ctx")
    chip, core = tm // 2, tm % 2
    place = jnp.where(core == 0, ctx // 4, ctx % 4)
    where = jnp.stack([place, core, chip]).astype(jnp.int32)
    latent = held(iterate[0])
    features, gap = frame_features(noise_steps[0])
    gap = jnp.pad(gap, (0, 128 - NF))[None, :]
    frame_row = held(frame_index[None, :])

    tie = lax.optimization_barrier
    mine, latent, frame_row = normed_pack(latent, frame_row, features, mod_weight)
    from_prev = send(mine, along("a", 1))
    from_next = send(mine, along("a", -1))
    from_far = send(mine, along("a", 2))
    lat_keep, lat_give = lat_terms(where, latent, frame_row, gap)
    lat_beside = send(lat_give, SWAP)
    gate, weight = side_terms(
        where, lat_give, frame_row, gap, features, mod_weight, qkv_weight
    )
    (lat_both,) = add_up(lat_keep, lat_beside, F32, weight)
    lat_got = send(lat_both, ROUND1)

    q0, kv0 = project(mine, from_prev, weight, after=(lat_both,))
    up0 = send(kv0, along("b", 1))
    down0 = send(kv0, along("b", -1))
    q1, kv1 = project(from_next, from_far, weight, after=(kv0,))
    down1 = send(kv1, along("b", -1))
    up1 = send(kv1, along("b", 1))
    far0 = send(up0, along("b", 1))
    state = attend([kv0, kv1, up0, down0], queries=(q0, q1))
    down1_later, _ = tie((down1, state[1]))
    far1 = send(down1_later, along("b", -1))
    state = attend([up1, down1], state=state)
    (lat_wire,) = add_up(lat_both, lat_got, F32, state[1])
    a1, a2, a3 = attend([far0, far1], state=state, last=(ROWS, 3 * ROWS), after=(lat_wire,))
    lat_far = send(lat_wire, ROUND2)
    b3 = send(a3, along("a", -2))
    b1 = send(a1, along("a", -1))
    b2 = send(a2, along("a", 1))
    (a0,) = attend([far0, far1], state=state, last=(0, ROWS), after=(a1,))
    part = out_first(where, a0, out_weight)
    pieces = (b1, b2, b3)
    give = out_rest(False, where, part, part, pieces, out_weight, gate)
    beside = send(give, SWAP)
    keep = out_rest(True, where, give, part, pieces, out_weight, gate)
    both, wire0, wire1 = add_up(keep, beside, BF16, keep, n_parts=2, keep=True)
    got0 = send(wire0, ROUND1)
    got1 = send(wire1, ROUND1)
    pair0 = pair_up(0, both, got0, wire0)
    far0 = send(pair0, ROUND2)
    pair1 = pair_up(1, both, got1, pair0)
    far1 = send(pair1, ROUND2)
    base_own, base_other, lat_sum = base_sum(
        where, pair1, anchor, lat_keep, lat_give, lat_beside, lat_got, lat_far
    )
    sum0 = back_sum(where, pair1, keep, got0, far0, lat_sum)
    back0 = send(sum0, SWAP)
    sum1 = back_sum(where, sum0, keep, got1, far1, lat_sum, QUART)
    back1 = send(sum1, SWAP)
    out = final_sum(True, (where, sum1, base_own, keep, beside, got0, got1, far0, far1))
    out = final_sum(False, (where, out, base_other, give, back0, back1))
    return out[None]


def solution(mesh):
    placed = (P("tm", "ctx", None), P("ctx", None), P("ctx"), P("tm", None), P(), P(), P())

    return jax.shard_map(
        per_device, mesh=mesh, in_specs=placed, out_specs=P("tm", "ctx", None), check_vma=False
    )
```

```python
import functools
import math

import jax
import jax.numpy as jnp
from jax import lax
from jax.experimental import pallas as pl
from jax.experimental.pallas import tpu as pltpu
from jax.sharding import PartitionSpec as P


HD = 128
NSCHED = 12
NF = 16
D = 1536
ROWS = 168
PACK = 176
WIDE = 384
PAIR = 2 * ROWS
PAIRPACK = PAIR + 8
QROWS = 4 * ROWS
HALF = D // 2
QUART = D // 4
BIG = 131072.0
AXES = ("tm", "ctx")

shift_factor = 5.0
norm_eps = 1e-06
F32 = jnp.float32
BF16 = jnp.bfloat16
VM = pl.BlockSpec(memory_space=pltpu.VMEM)
SM = pl.BlockSpec(memory_space=pltpu.SMEM)
ANY = pl.BlockSpec(memory_space=pl.ANY)
HBM = pl.BlockSpec(memory_space=pltpu.HBM)


def shaped(*shape, kind=F32):
    return jax.ShapeDtypeStruct(shape, kind)


def call(kernel, args, specs, outs, cost, scratch=(), mib=24, out_specs=None):
    flops, moved, exps = cost
    return run_kernel(kernel, args, specs, outs, flops, moved, exps, scratch, mib, out_specs)


def run_kernel(kernel, args, specs, outs, flops, moved, exps, scratch, mib, out_specs):
    return pl.pallas_call(
        kernel,
        in_specs=specs,
        out_specs=[VM] * len(outs) if out_specs is None else out_specs,
        out_shape=outs,
        scratch_shapes=list(scratch),
        compiler_params=pltpu.CompilerParams(vmem_limit_bytes=mib << 20),
        cost_estimate=pl.CostEstimate(flops=flops, bytes_accessed=moved, transcendentals=exps),
    )(*args)


def place_of(x, c, y, z):
    return ((x % 4) * 2 + c % 2) * 16 + (y % 4) * 4 + z % 4


def pairs(move):
    found = []
    for x in range(4):
        for c in range(2):
            for y in range(4):
                for z in range(4):
                    to = move(x, c, y, z)
                    if to is not None:
                        found.append((place_of(x, c, y, z), place_of(*to)))
    return found


def along(ring, step):
    def move(x, c, y, z):
        if (c == 0) == (ring == "a"):
            return (x, c, y + step, z)
        return (x, c, y, z + step)

    return pairs(move)


def send(value, route):
    return lax.ppermute(value, AXES, route)


def noise_level(level_index):
    fraction = level_index / NSCHED
    return shift_factor * fraction / (1.0 + (shift_factor - 1.0) * fraction)


def frame_features(steps_ref, rates_ref, feat_ref, gap_ref):
    level_row = steps_ref[...].astype(F32)
    gap_ref[...] = jnp.zeros((1, 128), F32)
    gap_ref[:, :NF] = noise_level(level_row + 1.0) - noise_level(level_row)
    level = jnp.broadcast_to(level_row, (128, NF)).T
    angles = (1000.0 * noise_level(level + 1.0)) * rates_ref[...]
    feat_ref[:, :128] = jnp.cos(angles).astype(BF16)
    feat_ref[:, 128:] = jnp.sin(angles).astype(BF16)


def split3(value):
    high = value.astype(BF16)
    rest = value - high.astype(F32)
    mid = rest.astype(BF16)
    low = (rest - mid.astype(F32)).astype(BF16)
    return jnp.concatenate([high, mid, low], axis=0)


def ones_by_frame(frame_row, rows):
    level = lax.broadcasted_iota(jnp.int32, (128, ROWS), 0)
    here = jnp.broadcast_to(frame_row, (128, ROWS))
    hit = jnp.where(jnp.logical_and(level % NF == here, level < rows), 1.0, 0.0)
    return hit.T


def pick_rows(ones, table):
    return jnp.dot(ones[:, : 3 * NF], split3(table), preferred_element_type=F32)


def norm_kernel(
    latent_hbm,
    frame_hbm,
    steps_hbm,
    rates_ref,
    mod_hbm,
    out_ref,
    lat_ref,
    frame_ref,
    feat_ref,
    gap_ref,
    mod_ref,
    picked_ref,
    unit_ref,
    steps_ref,
    sems,
):
    steps = pltpu.make_async_copy(steps_hbm, steps_ref, sems.at[7])
    steps.start()
    copies = [pltpu.make_async_copy(frame_hbm, frame_ref, sems.at[0])]
    for i in range(2):
        rows = pl.ds(i * (ROWS // 2 + 4), (88, 80)[i])
        copies.append(
            pltpu.make_async_copy(latent_hbm.at[rows, :], lat_ref.at[rows, :], sems.at[1 + i])
        )
    for i in range(4):
        cols = pl.ds(i * HALF, HALF)
        copies.append(pltpu.make_async_copy(mod_hbm.at[:, cols], mod_ref.at[:, cols], sems.at[3 + i]))
    for one in copies:
        one.start()
    copies[0].wait()
    ones = ones_by_frame(frame_ref[...], 3 * NF).astype(BF16)
    out_ref[ROWS:, :] = jnp.zeros((PACK - ROWS, D), BF16)
    out_ref[ROWS:, :ROWS] = jnp.broadcast_to(frame_ref[...], (8, ROWS)).astype(F32).astype(BF16)

    steps.wait()
    frame_features(steps_ref, rates_ref, feat_ref, gap_ref)

    def normal(i, carry):
        rows = pl.ds(pl.multiple_of(i * 8, 8), 8)
        latent = lat_ref[rows, :]
        center = latent - jnp.mean(latent, axis=-1, keepdims=True)
        spread = jnp.mean(center * center, axis=-1, keepdims=True)
        unit_ref[rows, :] = center * lax.rsqrt(spread + norm_eps)
        return carry

    copies[1].wait()
    lax.fori_loop(0, 11, normal, 0, unroll=True)
    copies[2].wait()
    lax.fori_loop(11, 21, normal, 0, unroll=True)
    for i in range(4):
        cols = pl.ds(i * HALF, HALF)
        copies[3 + i].wait()
        table = jnp.dot(feat_ref[...], mod_ref[:, cols], preferred_element_type=F32)
        picked = pick_rows(ones, table)
        if i < 2:
            picked_ref[:, cols] = picked
        else:
            cols = pl.ds((i - 2) * HALF, HALF)
            out = unit_ref[:, cols] * (1.0 + picked) + picked_ref[:, cols]
            out_ref[:ROWS, cols] = out.astype(BF16)


def normed_pack(latent, frame_row, steps_row, rates, mod_weight):
    return call(
        norm_kernel,
        (latent, frame_row, steps_row, rates, mod_weight),
        [HBM, HBM, HBM, VM, HBM],
        [
            shaped(PACK, D, kind=BF16),
            shaped(ROWS, D),
            shaped(1, ROWS, kind=jnp.int32),
            shaped(NF, 256, kind=BF16),
            shaped(1, 128),
        ],
        (30000000, 4000000, 0),
        [
            pltpu.VMEM((256, 2 * D), BF16),
            pltpu.VMEM((ROWS, D), F32),
            pltpu.VMEM((ROWS, D), F32),
            pltpu.VMEM((1, NF), jnp.int32),
            pltpu.SemaphoreType.DMA((8,)),
        ],
    )


def frame_gap(ones, gap_ref):
    return jnp.sum(ones[:, :NF] * gap_ref[:, :NF], axis=1, keepdims=True)


def lat_kernel(where_ref, latent_ref, frame_ref, gap_ref, keep_ref, give_ref):
    core = where_ref[1]
    gap = frame_gap(ones_by_frame(frame_ref[...], NF), gap_ref)
    mine = pl.ds(pl.multiple_of(core * HALF, 128), HALF)
    other = pl.ds(pl.multiple_of((1 - core) * HALF, 128), HALF)
    keep_ref[...] = -gap * latent_ref[:, mine]
    give_ref[...] = -gap * latent_ref[:, other]


def lat_terms(where, latent, frame_row, gap):
    return call(
        lat_kernel,
        (where, latent, frame_row, gap),
        [SM, VM, VM, VM],
        [shaped(ROWS, HALF), shaped(ROWS, HALF)],
        (ROWS * D, 2000000, 0),
    )


def side_kernel(
    where_ref, after_ref, frame_ref, gap_ref, feat_ref, mod_hbm, qkv_hbm, gate_ref, w_ref, mod_ref, sems
):
    place = where_ref[0]
    copies = [pltpu.make_async_copy(mod_hbm.at[:, pl.ds(2 * D, D)], mod_ref, sems.at[0])]
    for i in range(3):
        cols = pl.ds(pl.multiple_of(i * D + place * WIDE, 128), WIDE)
        copies.append(
            pltpu.make_async_copy(
                qkv_hbm.at[:, cols], w_ref.at[:, pl.ds(i * WIDE, WIDE)], sems.at[1 + i]
            )
        )
    for one in copies:
        one.start()
    ones = ones_by_frame(frame_ref[...], 3 * NF)
    gap = frame_gap(ones, gap_ref)
    copies[0].wait()
    table = jnp.dot(feat_ref[...], mod_ref[...], preferred_element_type=F32)
    gate_ref[...] = -gap * pick_rows(ones.astype(BF16), table)
    for one in copies[1:]:
        one.wait()


def side_terms(where, after, frame_row, gap, features, mod_weight, qkv_weight):
    return call(
        side_kernel,
        (where, after, frame_row, gap, features, mod_weight, qkv_weight),
        [SM, ANY, VM, VM, VM, HBM, HBM],
        [shaped(ROWS, D), shaped(D, 3 * WIDE, kind=BF16)],
        (30000000, 6000000, 0),
        [pltpu.VMEM((256, D), BF16), pltpu.SemaphoreType.DMA((4,))],
    )


def head_normed(one):
    mean = jnp.mean(one * one, axis=-1, keepdims=True)
    return (one * lax.rsqrt(mean + norm_eps)).astype(BF16)


def qkv_kernel(n_after, *refs):
    n0, n1, w_ref, q_ref, kv_ref, tok_ref = refs[n_after:]
    tok_ref[:ROWS, :] = n0[:ROWS, :]
    tok_ref[ROWS:, :] = n1[:ROWS, :]
    tokens = tok_ref[...]
    for h in range(3):
        cols = pl.ds(h * WIDE, WIDE)
        got = jnp.dot(tokens, w_ref[:, cols], preferred_element_type=F32)
        if h == 2:
            kv_ref[:PAIR, WIDE:] = got.astype(BF16)
            continue
        target = q_ref if h == 0 else kv_ref
        for i in range(3):
            part = pl.ds(i * HD, HD)
            target[:PAIR, part] = head_normed(got[:, i * HD : (i + 1) * HD])
    kv_ref[PAIR:, :256] = n0[ROWS:, :256]
    kv_ref[PAIR:, 256:512] = n1[ROWS:, :256]
    kv_ref[PAIR:, 512:] = jnp.zeros((8, 256), BF16)


def project(n0, n1, weight, after=()):
    return call(
        functools.partial(qkv_kernel, len(after)),
        (*after, n0, n1, weight),
        [ANY] * len(after) + [VM] * 3,
        [shaped(PAIR, WIDE, kind=BF16), shaped(PAIRPACK, 2 * WIDE, kind=BF16)],
        (2 * PAIR * D * 3 * WIDE, 5000000, 0),
        [pltpu.VMEM((PAIR, D), BF16)],
    )


def lanes_to_rows(pack_ref, put, make):
    for i in range(2):
        here = pack_ref[PAIR : PAIR + 1, i * 256 : (i + 1) * 256].astype(F32)
        level = lax.broadcasted_iota(jnp.int32, (HD, 256), 0).astype(F32)
        put(i, make(level, here).T[:ROWS].astype(BF16))


def attend_kernel(n_after, n_kv, first, last, row0, nrows, *refs):
    refs = list(refs)[n_after:]
    if first:
        q0, q1, kvs, rest = refs[0], refs[1], refs[2 : 2 + n_kv], refs[2 + n_kv :]
        num_ref, den_ref, qx_ref, key_ref, val_ref = rest
        for j, (q_ref, kv_ref) in enumerate(((q0, kvs[0]), (q1, kvs[1]))):
            rows = pl.ds(j * PAIR, PAIR)
            for h in range(3):
                qx_ref[rows, pl.ds(h * 256, HD)] = q_ref[:, pl.ds(h * HD, HD)]

            def put(i, block):
                at = pl.ds(j * PAIR + i * ROWS, ROWS)
                for h in range(3):
                    qx_ref[at, pl.ds(h * 256 + HD, HD)] = block

            lanes_to_rows(kv_ref, put, lambda level, here: jnp.where(level > here, -BIG, 0.0))
    else:
        qx_ref, num_in, den_in, kvs, rest = refs[0], refs[1], refs[2], refs[3 : 3 + n_kv], refs[3 + n_kv :]
        if last:
            outs, (key_ref, val_ref) = rest[:-2], rest[-2:]
        else:
            num_ref, den_ref, key_ref, val_ref = rest

    for j, kv_ref in enumerate(kvs):
        rows = pl.ds(j * PAIR, PAIR)
        for h in range(3):
            key_ref[rows, pl.ds(h * 256, HD)] = kv_ref[:PAIR, pl.ds(h * HD, HD)]
        val_ref[rows, :] = kv_ref[:PAIR, WIDE:]

        def put(i, block):
            at = pl.ds(j * PAIR + i * ROWS, ROWS)
            for h in range(3):
                key_ref[at, pl.ds(h * 256 + HD, HD)] = block

        lanes_to_rows(kv_ref, put, lambda level, here: jnp.where(level == here, 1.0, 0.0))
    used, whole_keys = n_kv * PAIR, key_ref.shape[0]
    extra = pl.ds(used, whole_keys - used)
    column = lax.broadcasted_iota(jnp.int32, (whole_keys - used, HD), 1)
    last_frame = jnp.where(column == NF, 1.0, 0.0).astype(BF16)
    for h in range(3):
        key_ref[extra, pl.ds(h * 256, HD)] = jnp.zeros((whole_keys - used, HD), BF16)
        key_ref[extra, pl.ds(h * 256 + HD, HD)] = last_frame
    val_ref[extra, :] = jnp.zeros((whole_keys - used, WIDE), BF16)

    scale = HD**-0.5 * math.log2(math.e)
    rows = pl.ds(row0, nrows)
    for h in range(3):
        cols = pl.ds(h * HD, HD)
        wide = pl.ds(h * 256, 256)
        scores = lax.dot_general(
            qx_ref[rows, wide], key_ref[:, wide], (((1,), (1,)), ((), ())),
            preferred_element_type=F32,
        )
        weights = jnp.exp2(scores * scale)
        den = weights[:, :HD]
        for i in range(1, whole_keys // HD):
            den = den + weights[:, i * HD : (i + 1) * HD]
        num = jnp.dot(weights.astype(BF16), val_ref[:, cols], preferred_element_type=F32)
        if not first:
            num = num + num_in[rows, cols]
            den = den + den_in[rows, cols]
        if last:
            done = (num / jnp.sum(den, axis=1, keepdims=True)).astype(BF16)
            for i, out_ref in enumerate(outs):
                out_ref[:, cols] = done[i * ROWS : (i + 1) * ROWS]
        else:
            num_ref[:, cols] = num
            den_ref[:, cols] = den


def attend(kvs, queries=None, state=None, last=None, after=()):
    n_kv = len(kvs)
    first = state is None
    row0, nrows = (0, QROWS) if last is None else last
    args = (list(queries) if first else list(state)) + list(kvs)
    if last is None:
        outs = [shaped(QROWS, WIDE), shaped(QROWS, WIDE)]
        if first:
            outs.append(shaped(QROWS, 768, kind=BF16))
    else:
        outs = [shaped(ROWS, WIDE, kind=BF16)] * (nrows // ROWS)
    got = call(
        functools.partial(attend_kernel, len(after), n_kv, first, last is not None, row0, nrows),
        list(after) + args,
        [ANY] * len(after) + [VM] * len(args),
        outs,
        (4 * nrows * PAIR * n_kv * WIDE * 2, 2000000, nrows * PAIR * 3 * n_kv),
        [
            pltpu.VMEM((-(-n_kv * PAIR // HD) * HD, 768), BF16),
            pltpu.VMEM((-(-n_kv * PAIR // HD) * HD, WIDE), BF16),
        ],
    )
    if last is not None:
        return got
    return (got[2] if first else state[0], got[0], got[1])


def out_rows(where_ref, step):
    return pl.ds(pl.multiple_of(lax.rem(where_ref[0] + step, 4) * WIDE, 128), WIDE)


def out_first_kernel(where_ref, a_ref, w_ref, part_ref):
    part_ref[...] = jnp.dot(a_ref[...], w_ref[out_rows(where_ref, 0), :], preferred_element_type=F32)


def out_first(where, piece, out_weight):
    return call(
        out_first_kernel,
        (where, piece, out_weight),
        [SM, VM, VM],
        [shaped(ROWS, D)],
        (2 * ROWS * WIDE * D, 5000000, 0),
    )[0]


def out_rest_kernel(own, where_ref, after_ref, part_ref, a1, a2, a3, w_ref, gate_ref, term_ref):
    core = where_ref[1]
    half = core if own else 1 - core
    cols = pl.ds(pl.multiple_of(half * HALF, 128), HALF)
    branch = part_ref[:, cols]
    for piece, step in ((a1, 1), (a2, 3), (a3, 2)):
        weight = w_ref[out_rows(where_ref, step), cols]
        branch = branch + jnp.dot(piece[...], weight, preferred_element_type=F32)
    term_ref[...] = gate_ref[:, cols] * branch


def out_rest(own, where, after, part, pieces, out_weight, gate):
    return call(
        functools.partial(out_rest_kernel, own),
        (where, after, part, *pieces, out_weight, gate),
        [SM, ANY] + [VM] * 6,
        [shaped(ROWS, HALF)],
        (ROWS * 3 * WIDE * D, 5000000, 0),
    )[0]


def add_kernel(n_parts, a_ref, b_ref, after_ref, *outs):
    total = a_ref[...] + b_ref[...].astype(F32)
    if len(outs) > n_parts:
        outs[0][...] = total
    wide = total.shape[1] // n_parts
    for i, wire_ref in enumerate(outs[-n_parts:]):
        wire_ref[...] = total[:, i * wide : (i + 1) * wide].astype(wire_ref.dtype)


def add_up(a, b, wire, after, n_parts=1, keep=False):
    wide = a.shape[1]
    outs = [shaped(ROWS, wide // n_parts, kind=wire)] * n_parts
    return call(
        functools.partial(add_kernel, n_parts),
        (a, b, after),
        [VM, VM, ANY],
        ([shaped(ROWS, wide)] if keep else []) + outs,
        (ROWS * wide, 2000000, 0),
    )


def pair_kernel(part, both_ref, got_ref, after_ref, wire_ref):
    total = both_ref[:, pl.ds(part * QUART, QUART)] + got_ref[...].astype(F32)
    wire_ref[...] = total.astype(wire_ref.dtype)


def pair_up(part, both, got, after):
    return call(
        functools.partial(pair_kernel, part),
        (both, got, after),
        [VM, VM, ANY],
        [shaped(ROWS, QUART, kind=BF16)],
        (ROWS * QUART, 1000000, 0),
    )[0]


def before_sum(where_ref, got_ref, far_ref):
    chip = where_ref[2]
    near = jnp.where(lax.rem(chip, 2) == 1, got_ref[...].astype(F32), 0.0)
    return near + jnp.where(chip >= 2, far_ref[...].astype(F32), 0.0)


def back_kernel(col0, where_ref, keep_ref, got_ref, far_ref, lat_ref, out_ref):
    cols = pl.ds(col0, got_ref.shape[1])
    extra = jnp.where(where_ref[1] == 0, keep_ref[:, cols], 0.0) + lat_ref[:, cols]
    out_ref[...] = before_sum(where_ref, got_ref, far_ref) + extra


def back_sum(where, after, keep, got, far, lat, col0=0):
    return call(
        lambda _, *refs: back_kernel(col0, *refs),
        (after, where, keep, got, far, lat),
        [ANY, SM] + [VM] * 4,
        [shaped(*got.shape)],
        (ROWS * HALF, 2000000, 0),
    )[0]


def base_kernel(
    where_ref, after_ref, anchor_ref, keep_ref, give_ref, beside_ref, got_ref, far_ref, own_ref, other_ref, back_ref
):
    core = where_ref[1]
    mine = pl.ds(pl.multiple_of(core * HALF, 128), HALF)
    other = pl.ds(pl.multiple_of((1 - core) * HALF, 128), HALF)
    before = before_sum(where_ref, got_ref, far_ref)
    own = before + jnp.where(core == 1, beside_ref[...], 0.0)
    own_ref[...] = anchor_ref[:, mine] + (keep_ref[...] + own)
    other_ref[...] = anchor_ref[:, other] + give_ref[...]
    back_ref[...] = before + jnp.where(core == 0, keep_ref[...], 0.0)


def base_sum(where, after, *terms):
    return call(
        base_kernel,
        (where, after, *terms),
        [SM, ANY] + [VM] * 6,
        [shaped(ROWS, HALF)] * 3,
        (ROWS * D * 2, 4000000, 0),
    )


def final_kernel(own, where_ref, *refs):
    core = where_ref[1]
    if own:
        _, base_ref, keep_ref, beside_ref, g0, g1, f0, f1, out_hbm, buf_ref, sems = refs
    else:
        _, base_ref, give_ref, b0, b1, out_hbm, buf_ref, sems = refs
    half = core if own else 1 - core
    copies = []
    for i in range(2):
        part = pl.ds(i * QUART, QUART)
        at = pl.ds(pl.multiple_of(half * HALF + i * QUART, 128), QUART)
        if own:
            got, far = ((g0, f0), (g1, f1))[i]
            more = before_sum(where_ref, got, far) + jnp.where(core == 1, beside_ref[:, part], 0.0)
            term = keep_ref[:, part] + more
        else:
            term = give_ref[:, part] + (b0, b1)[i][...]
        buf_ref[:, part] = base_ref[:, part] + term
        copies.append(pltpu.make_async_copy(buf_ref.at[:, part], out_hbm.at[:, at], sems.at[i]))
        copies[-1].start()
    for one in copies:
        one.wait()


def final_sum(own, args):
    n = len(args)
    return pl.pallas_call(
        functools.partial(final_kernel, own),
        in_specs=[SM, HBM if not own else ANY] + [VM] * (n - 2),
        out_specs=HBM,
        out_shape=shaped(ROWS, D),
        input_output_aliases={} if own else {1: 0},
        scratch_shapes=[pltpu.VMEM((ROWS, HALF), F32), pltpu.SemaphoreType.DMA((2,))],
        compiler_params=pltpu.CompilerParams(vmem_limit_bytes=24 << 20),
        cost_estimate=pl.CostEstimate(flops=ROWS * D, bytes_accessed=2000000, transcendentals=0),
        name="final_own" if own else "final_other",
    )(*args)


SWAP = pairs(lambda x, c, y, z: (x, 1 - c, y, z))
ROUND1 = pairs(lambda x, c, y, z: (x ^ 1, c, y, z))
ROUND2 = pairs(lambda x, c, y, z: (3 - x, c, y, z) if x < 2 else None)


def held(x):
    return pltpu.with_memory_space_constraint(x, pltpu.HBM)


def per_device(iterate, anchor, frame_index, noise_steps, qkv_weight, out_weight, mod_weight):
    qkv_weight, mod_weight = held(qkv_weight), held(mod_weight)
    tm = lax.axis_index("tm")
    ctx = lax.axis_index("ctx")
    chip, core = tm // 2, tm % 2
    place = jnp.where(core == 0, ctx // 4, ctx % 4)
    where = jnp.stack([place, core, chip]).astype(jnp.int32)
    latent = held(iterate[0])
    rates = jnp.exp(-math.log(10000.0) * jnp.arange(128, dtype=F32) / 128)[None, :]
    frame_row = held(frame_index[None, :])

    tie = lax.optimization_barrier
    mine, latent, frame_row, features, gap = normed_pack(
        latent, frame_row, held(noise_steps), rates, mod_weight
    )
    from_prev = send(mine, along("a", 1))
    from_next = send(mine, along("a", -1))
    from_far = send(mine, along("a", 2))
    lat_keep, lat_give = lat_terms(where, latent, frame_row, gap)
    lat_beside = send(lat_give, SWAP)
    gate, weight = side_terms(
        where, lat_give, frame_row, gap, features, mod_weight, qkv_weight
    )
    (lat_both,) = add_up(lat_keep, lat_beside, F32, weight)
    lat_got = send(lat_both, ROUND1)

    q0, kv0 = project(mine, from_prev, weight, after=(lat_both,))
    up0 = send(kv0, along("b", 1))
    down0 = send(kv0, along("b", -1))
    q1, kv1 = project(from_next, from_far, weight, after=(kv0,))
    down1 = send(kv1, along("b", -1))
    up1 = send(kv1, along("b", 1))
    far0 = send(up0, along("b", 1))
    state = attend([kv0, kv1, up0, down0], queries=(q0, q1))
    down1_later, _ = tie((down1, state[1]))
    far1 = send(down1_later, along("b", -1))
    state = attend([up1, down1], state=state)
    (lat_wire,) = add_up(lat_both, lat_got, F32, state[1])
    a1, a2, a3 = attend([far0, far1], state=state, last=(ROWS, 3 * ROWS), after=(lat_wire,))
    lat_far = send(lat_wire, ROUND2)
    b3 = send(a3, along("a", -2))
    b1 = send(a1, along("a", -1))
    b2 = send(a2, along("a", 1))
    (a0,) = attend([far0, far1], state=state, last=(0, ROWS), after=(a1,))
    part = out_first(where, a0, out_weight)
    pieces = (b1, b2, b3)
    give = out_rest(False, where, part, part, pieces, out_weight, gate)
    beside = send(give, SWAP)
    keep = out_rest(True, where, give, part, pieces, out_weight, gate)
    both, wire0, wire1 = add_up(keep, beside, BF16, keep, n_parts=2, keep=True)
    got0 = send(wire0, ROUND1)
    got1 = send(wire1, ROUND1)
    pair0 = pair_up(0, both, got0, wire0)
    far0 = send(pair0, ROUND2)
    pair1 = pair_up(1, both, got1, pair0)
    far1 = send(pair1, ROUND2)
    base_own, base_other, lat_sum = base_sum(
        where, pair1, anchor, lat_keep, lat_give, lat_beside, lat_got, lat_far
    )
    sum0 = back_sum(where, pair1, keep, got0, far0, lat_sum)
    back0 = send(sum0, SWAP)
    sum1 = back_sum(where, sum0, keep, got1, far1, lat_sum, QUART)
    back1 = send(sum1, SWAP)
    out = final_sum(True, (where, sum1, base_own, keep, beside, got0, got1, far0, far1))
    out = final_sum(False, (where, out, base_other, give, back0, back1))
    return out[None]


def solution(mesh):
    placed = (P("tm", "ctx", None), P("ctx", None), P("ctx"), P("tm", None), P(), P(), P())

    return jax.shard_map(
        per_device, mesh=mesh, in_specs=placed, out_specs=P("tm", "ctx", None), check_vma=False
    )
```

```python
import functools
import math

import jax
import jax.numpy as jnp
from jax import lax
from jax.experimental import pallas as pl
from jax.experimental.pallas import tpu as pltpu
from jax.sharding import PartitionSpec as P


HD = 128
NSCHED = 12
NF = 16
D = 1536
ROWS = 168
PACK = 176
WIDE = 384
PAIR = 2 * ROWS
PAIRPACK = PAIR + 8
QROWS = 4 * ROWS
HALF = D // 2
QUART = D // 4
BIG = 131072.0
AXES = ("tm", "ctx")

shift_factor = 5.0
norm_eps = 1e-06
F32 = jnp.float32
BF16 = jnp.bfloat16
VM = pl.BlockSpec(memory_space=pltpu.VMEM)
SM = pl.BlockSpec(memory_space=pltpu.SMEM)
ANY = pl.BlockSpec(memory_space=pl.ANY)
HBM = pl.BlockSpec(memory_space=pltpu.HBM)


def shaped(*shape, kind=F32):
    return jax.ShapeDtypeStruct(shape, kind)


def call(kernel, args, specs, outs, cost, scratch=(), mib=24, out_specs=None):
    flops, moved, exps = cost
    return run_kernel(kernel, args, specs, outs, flops, moved, exps, scratch, mib, out_specs)


def run_kernel(kernel, args, specs, outs, flops, moved, exps, scratch, mib, out_specs):
    return pl.pallas_call(
        kernel,
        in_specs=specs,
        out_specs=[VM] * len(outs) if out_specs is None else out_specs,
        out_shape=outs,
        scratch_shapes=list(scratch),
        compiler_params=pltpu.CompilerParams(vmem_limit_bytes=mib << 20),
        cost_estimate=pl.CostEstimate(flops=flops, bytes_accessed=moved, transcendentals=exps),
    )(*args)


def place_of(x, c, y, z):
    return ((x % 4) * 2 + c % 2) * 16 + (y % 4) * 4 + z % 4


def pairs(move):
    found = []
    for x in range(4):
        for c in range(2):
            for y in range(4):
                for z in range(4):
                    to = move(x, c, y, z)
                    if to is not None:
                        found.append((place_of(x, c, y, z), place_of(*to)))
    return found


def along(ring, step):
    def move(x, c, y, z):
        if (c == 0) == (ring == "a"):
            return (x, c, y + step, z)
        return (x, c, y, z + step)

    return pairs(move)


def exchange(ring, kind):
    def partner(p):
        return p ^ 1 if kind == 1 else 3 - p

    def move(x, c, y, z):
        if (c == 0) == (ring == "a"):
            return (x, c, partner(y), z)
        return (x, c, y, partner(z))

    return pairs(move)


def send(value, route):
    return lax.ppermute(value, AXES, route)


def noise_level(level_index):
    fraction = level_index / NSCHED
    return shift_factor * fraction / (1.0 + (shift_factor - 1.0) * fraction)


def frame_features(steps_ref, rates_ref, feat_ref, gap_ref):
    level_row = steps_ref[...].astype(F32)
    gap_ref[...] = jnp.zeros((1, 128), F32)
    gap_ref[:, :NF] = noise_level(level_row + 1.0) - noise_level(level_row)
    level = jnp.broadcast_to(level_row, (128, NF)).T
    angles = (1000.0 * noise_level(level + 1.0)) * rates_ref[...]
    feat_ref[:, :128] = jnp.cos(angles).astype(BF16)
    feat_ref[:, 128:] = jnp.sin(angles).astype(BF16)


def split3(value):
    high = value.astype(BF16)
    rest = value - high.astype(F32)
    mid = rest.astype(BF16)
    low = (rest - mid.astype(F32)).astype(BF16)
    return jnp.concatenate([high, mid, low], axis=0)


def ones_by_frame(frame_row, rows):
    level = lax.broadcasted_iota(jnp.int32, (128, ROWS), 0)
    here = jnp.broadcast_to(frame_row, (128, ROWS))
    hit = jnp.where(jnp.logical_and(level % NF == here, level < rows), 1.0, 0.0)
    return hit.T


def pick_rows(ones, table):
    return jnp.dot(ones[:, : 3 * NF], split3(table), preferred_element_type=F32)


def norm_kernel(
    latent_hbm,
    frame_hbm,
    steps_hbm,
    rates_ref,
    mod_hbm,
    out_ref,
    lat_ref,
    frame_ref,
    feat_ref,
    gap_ref,
    mod_ref,
    picked_ref,
    unit_ref,
    steps_ref,
    sems,
):
    steps = pltpu.make_async_copy(steps_hbm, steps_ref, sems.at[7])
    steps.start()
    copies = [pltpu.make_async_copy(frame_hbm, frame_ref, sems.at[0])]
    for i in range(2):
        rows = pl.ds(i * (ROWS // 2 + 4), (88, 80)[i])
        copies.append(
            pltpu.make_async_copy(latent_hbm.at[rows, :], lat_ref.at[rows, :], sems.at[1 + i])
        )
    for i in range(4):
        cols = pl.ds(i * HALF, HALF)
        copies.append(pltpu.make_async_copy(mod_hbm.at[:, cols], mod_ref.at[:, cols], sems.at[3 + i]))
    for one in copies:
        one.start()
    copies[0].wait()
    ones = ones_by_frame(frame_ref[...], 3 * NF).astype(BF16)
    out_ref[ROWS:, :] = jnp.zeros((PACK - ROWS, D), BF16)
    out_ref[ROWS:, :ROWS] = jnp.broadcast_to(frame_ref[...], (8, ROWS)).astype(F32).astype(BF16)

    steps.wait()
    frame_features(steps_ref, rates_ref, feat_ref, gap_ref)

    def normal(i, carry):
        rows = pl.ds(pl.multiple_of(i * 8, 8), 8)
        latent = lat_ref[rows, :]
        center = latent - jnp.mean(latent, axis=-1, keepdims=True)
        spread = jnp.mean(center * center, axis=-1, keepdims=True)
        unit_ref[rows, :] = center * lax.rsqrt(spread + norm_eps)
        return carry

    copies[1].wait()
    lax.fori_loop(0, 11, normal, 0, unroll=True)
    copies[2].wait()
    lax.fori_loop(11, 21, normal, 0, unroll=True)
    for i in range(4):
        cols = pl.ds(i * HALF, HALF)
        copies[3 + i].wait()
        table = jnp.dot(feat_ref[...], mod_ref[:, cols], preferred_element_type=F32)
        picked = pick_rows(ones, table)
        if i < 2:
            picked_ref[:, cols] = picked
        else:
            cols = pl.ds((i - 2) * HALF, HALF)
            out = unit_ref[:, cols] * (1.0 + picked) + picked_ref[:, cols]
            out_ref[:ROWS, cols] = out.astype(BF16)


def normed_pack(latent, frame_row, steps_row, rates, mod_weight):
    return call(
        norm_kernel,
        (latent, frame_row, steps_row, rates, mod_weight),
        [HBM, HBM, HBM, VM, HBM],
        [
            shaped(PACK, D, kind=BF16),
            shaped(ROWS, D),
            shaped(1, ROWS, kind=jnp.int32),
            shaped(NF, 256, kind=BF16),
            shaped(1, 128),
        ],
        (30000000, 4000000, 0),
        [
            pltpu.VMEM((256, 2 * D), BF16),
            pltpu.VMEM((ROWS, D), F32),
            pltpu.VMEM((ROWS, D), F32),
            pltpu.VMEM((1, NF), jnp.int32),
            pltpu.SemaphoreType.DMA((8,)),
        ],
    )


def frame_gap(ones, gap_ref):
    return jnp.sum(ones[:, :NF] * gap_ref[:, :NF], axis=1, keepdims=True)


def lat_kernel(where_ref, latent_ref, frame_ref, gap_ref, keep_ref, give_ref):
    core = where_ref[1]
    gap = frame_gap(ones_by_frame(frame_ref[...], NF), gap_ref)
    mine = pl.ds(pl.multiple_of(core * HALF, 128), HALF)
    other = pl.ds(pl.multiple_of((1 - core) * HALF, 128), HALF)
    keep_ref[...] = -gap * latent_ref[:, mine]
    give_ref[...] = -gap * latent_ref[:, other]


def lat_terms(where, latent, frame_row, gap):
    return call(
        lat_kernel,
        (where, latent, frame_row, gap),
        [SM, VM, VM, VM],
        [shaped(ROWS, HALF), shaped(ROWS, HALF)],
        (ROWS * D, 2000000, 0),
    )


def side_kernel(
    where_ref, after_ref, frame_ref, gap_ref, feat_ref, mod_hbm, qkv_hbm, gate_ref, w_ref, mod_ref, sems
):
    place = where_ref[0]
    copies = [pltpu.make_async_copy(mod_hbm.at[:, pl.ds(2 * D, D)], mod_ref, sems.at[0])]
    for i in range(3):
        cols = pl.ds(pl.multiple_of(i * D + place * WIDE, 128), WIDE)
        copies.append(
            pltpu.make_async_copy(
                qkv_hbm.at[:, cols], w_ref.at[:, pl.ds(i * WIDE, WIDE)], sems.at[1 + i]
            )
        )
    for one in copies:
        one.start()
    ones = ones_by_frame(frame_ref[...], 3 * NF)
    gap = frame_gap(ones, gap_ref)
    copies[0].wait()
    table = jnp.dot(feat_ref[...], mod_ref[...], preferred_element_type=F32)
    gate_ref[...] = -gap * pick_rows(ones.astype(BF16), table)
    for one in copies[1:]:
        one.wait()


def side_terms(where, after, frame_row, gap, features, mod_weight, qkv_weight):
    return call(
        side_kernel,
        (where, after, frame_row, gap, features, mod_weight, qkv_weight),
        [SM, ANY, VM, VM, VM, HBM, HBM],
        [shaped(ROWS, D), shaped(D, 3 * WIDE, kind=BF16)],
        (30000000, 6000000, 0),
        [pltpu.VMEM((256, D), BF16), pltpu.SemaphoreType.DMA((4,))],
    )


def head_normed(one):
    mean = jnp.mean(one * one, axis=-1, keepdims=True)
    return (one * lax.rsqrt(mean + norm_eps)).astype(BF16)


def qkv_kernel(n_after, *refs):
    n0, n1, w_ref, q_ref, kv_ref, tok_ref = refs[n_after:]
    tok_ref[:ROWS, :] = n0[:ROWS, :]
    tok_ref[ROWS:, :] = n1[:ROWS, :]
    tokens = tok_ref[...]
    for h in range(3):
        cols = pl.ds(h * WIDE, WIDE)
        got = jnp.dot(tokens, w_ref[:, cols], preferred_element_type=F32)
        if h == 2:
            kv_ref[:PAIR, WIDE:] = got.astype(BF16)
            continue
        target = q_ref if h == 0 else kv_ref
        for i in range(3):
            part = pl.ds(i * HD, HD)
            target[:PAIR, part] = head_normed(got[:, i * HD : (i + 1) * HD])
    kv_ref[PAIR:, :256] = n0[ROWS:, :256]
    kv_ref[PAIR:, 256:512] = n1[ROWS:, :256]
    kv_ref[PAIR:, 512:] = jnp.zeros((8, 256), BF16)


def project(n0, n1, weight, after=()):
    return call(
        functools.partial(qkv_kernel, len(after)),
        (*after, n0, n1, weight),
        [ANY] * len(after) + [VM] * 3,
        [shaped(PAIR, WIDE, kind=BF16), shaped(PAIRPACK, 2 * WIDE, kind=BF16)],
        (2 * PAIR * D * 3 * WIDE, 5000000, 0),
        [pltpu.VMEM((PAIR, D), BF16)],
    )


def lanes_to_rows(pack_ref, put, make):
    for i in range(2):
        here = pack_ref[PAIR : PAIR + 1, i * 256 : (i + 1) * 256].astype(F32)
        level = lax.broadcasted_iota(jnp.int32, (HD, 256), 0).astype(F32)
        put(i, make(level, here).T[:ROWS].astype(BF16))


def attend_kernel(n_after, n_kv, first, last, row0, nrows, *refs):
    refs = list(refs)[n_after:]
    if first:
        q0, q1, kvs, rest = refs[0], refs[1], refs[2 : 2 + n_kv], refs[2 + n_kv :]
        num_ref, den_ref, qx_ref, key_ref, val_ref = rest
        for j, (q_ref, kv_ref) in enumerate(((q0, kvs[0]), (q1, kvs[1]))):
            rows = pl.ds(j * PAIR, PAIR)
            for h in range(3):
                qx_ref[rows, pl.ds(h * 256, HD)] = q_ref[:, pl.ds(h * HD, HD)]

            def put(i, block):
                at = pl.ds(j * PAIR + i * ROWS, ROWS)
                for h in range(3):
                    qx_ref[at, pl.ds(h * 256 + HD, HD)] = block

            lanes_to_rows(kv_ref, put, lambda level, here: jnp.where(level > here, -BIG, 0.0))
    else:
        qx_ref, num_in, den_in, kvs, rest = refs[0], refs[1], refs[2], refs[3 : 3 + n_kv], refs[3 + n_kv :]
        if last:
            outs, (key_ref, val_ref) = rest[:-2], rest[-2:]
        else:
            num_ref, den_ref, key_ref, val_ref = rest

    for j, kv_ref in enumerate(kvs):
        rows = pl.ds(j * PAIR, PAIR)
        for h in range(3):
            key_ref[rows, pl.ds(h * 256, HD)] = kv_ref[:PAIR, pl.ds(h * HD, HD)]
        val_ref[rows, :] = kv_ref[:PAIR, WIDE:]

        def put(i, block):
            at = pl.ds(j * PAIR + i * ROWS, ROWS)
            for h in range(3):
                key_ref[at, pl.ds(h * 256 + HD, HD)] = block

        lanes_to_rows(kv_ref, put, lambda level, here: jnp.where(level == here, 1.0, 0.0))
    used, whole_keys = n_kv * PAIR, key_ref.shape[0]
    extra = pl.ds(used, whole_keys - used)
    column = lax.broadcasted_iota(jnp.int32, (whole_keys - used, HD), 1)
    last_frame = jnp.where(column == NF, 1.0, 0.0).astype(BF16)
    for h in range(3):
        key_ref[extra, pl.ds(h * 256, HD)] = jnp.zeros((whole_keys - used, HD), BF16)
        key_ref[extra, pl.ds(h * 256 + HD, HD)] = last_frame
    val_ref[extra, :] = jnp.zeros((whole_keys - used, WIDE), BF16)

    scale = HD**-0.5 * math.log2(math.e)
    rows = pl.ds(row0, nrows)
    for h in range(3):
        cols = pl.ds(h * HD, HD)
        wide = pl.ds(h * 256, 256)
        scores = lax.dot_general(
            qx_ref[rows, wide], key_ref[:, wide], (((1,), (1,)), ((), ())),
            preferred_element_type=F32,
        )
        weights = jnp.exp2(scores * scale)
        den = weights[:, :HD]
        for i in range(1, whole_keys // HD):
            den = den + weights[:, i * HD : (i + 1) * HD]
        num = jnp.dot(weights.astype(BF16), val_ref[:, cols], preferred_element_type=F32)
        if not first:
            num = num + num_in[rows, cols]
            den = den + den_in[rows, cols]
        if last:
            done = (num / jnp.sum(den, axis=1, keepdims=True)).astype(BF16)
            for i, out_ref in enumerate(outs):
                out_ref[:, cols] = done[i * ROWS : (i + 1) * ROWS]
        else:
            num_ref[:, cols] = num
            den_ref[:, cols] = den


def attend(kvs, queries=None, state=None, last=None, after=()):
    n_kv = len(kvs)
    first = state is None
    row0, nrows = (0, QROWS) if last is None else last
    args = (list(queries) if first else list(state)) + list(kvs)
    if last is None:
        outs = [shaped(QROWS, WIDE), shaped(QROWS, WIDE)]
        if first:
            outs.append(shaped(QROWS, 768, kind=BF16))
    else:
        outs = [shaped(ROWS, WIDE, kind=BF16)] * (nrows // ROWS)
    got = call(
        functools.partial(attend_kernel, len(after), n_kv, first, last is not None, row0, nrows),
        list(after) + args,
        [ANY] * len(after) + [VM] * len(args),
        outs,
        (4 * nrows * PAIR * n_kv * WIDE * 2, 2000000, nrows * PAIR * 3 * n_kv),
        [
            pltpu.VMEM((-(-n_kv * PAIR // HD) * HD, 768), BF16),
            pltpu.VMEM((-(-n_kv * PAIR // HD) * HD, WIDE), BF16),
        ],
    )
    if last is not None:
        return got
    return (got[2] if first else state[0], got[0], got[1])


def out_rows(group):
    return pl.ds(pl.multiple_of(group * WIDE, 128), WIDE)


def out_first_kernel(where_ref, a_ref, w_ref, part_ref):
    part_ref[...] = jnp.dot(a_ref[...], w_ref[out_rows(where_ref[0]), :], preferred_element_type=F32)


def out_first(where, piece, out_weight):
    return call(
        out_first_kernel,
        (where, piece, out_weight),
        [SM, VM, VM],
        [shaped(ROWS, D)],
        (2 * ROWS * WIDE * D, 5000000, 0),
    )[0]


def out_rest_kernel(own, where_ref, after_ref, part_ref, a1, a2, a3, w_ref, gate_ref, term_ref):
    core = where_ref[1]
    half = core if own else 1 - core
    cols = pl.ds(pl.multiple_of(half * HALF, 128), HALF)
    branch = part_ref[:, cols]
    place = where_ref[0]
    near = place + 1 - 2 * lax.rem(place, 2)
    for piece, group in ((a1, near), (a2, 3 - place), (a3, lax.rem(place + 2, 4))):
        weight = w_ref[out_rows(group), cols]
        branch = branch + jnp.dot(piece[...], weight, preferred_element_type=F32)
    term_ref[...] = gate_ref[:, cols] * branch


def out_rest(own, where, after, part, pieces, out_weight, gate):
    return call(
        functools.partial(out_rest_kernel, own),
        (where, after, part, *pieces, out_weight, gate),
        [SM, ANY] + [VM] * 6,
        [shaped(ROWS, HALF)],
        (ROWS * 3 * WIDE * D, 5000000, 0),
    )[0]


def add_kernel(n_parts, a_ref, b_ref, after_ref, *outs):
    total = a_ref[...] + b_ref[...].astype(F32)
    if len(outs) > n_parts:
        outs[0][...] = total
    wide = total.shape[1] // n_parts
    for i, wire_ref in enumerate(outs[-n_parts:]):
        wire_ref[...] = total[:, i * wide : (i + 1) * wide].astype(wire_ref.dtype)


def add_up(a, b, wire, after, n_parts=1, keep=False):
    wide = a.shape[1]
    outs = [shaped(ROWS, wide // n_parts, kind=wire)] * n_parts
    return call(
        functools.partial(add_kernel, n_parts),
        (a, b, after),
        [VM, VM, ANY],
        ([shaped(ROWS, wide)] if keep else []) + outs,
        (ROWS * wide, 2000000, 0),
    )


def pair_kernel(part, both_ref, got_ref, after_ref, wire_ref):
    total = both_ref[:, pl.ds(part * QUART, QUART)] + got_ref[...].astype(F32)
    wire_ref[...] = total.astype(wire_ref.dtype)


def pair_up(part, both, got, after):
    return call(
        functools.partial(pair_kernel, part),
        (both, got, after),
        [VM, VM, ANY],
        [shaped(ROWS, QUART, kind=BF16)],
        (ROWS * QUART, 1000000, 0),
    )[0]


def before_sum(where_ref, got_ref, far_ref):
    chip = where_ref[2]
    near = jnp.where(lax.rem(chip, 2) == 1, got_ref[...].astype(F32), 0.0)
    return near + jnp.where(chip >= 2, far_ref[...].astype(F32), 0.0)


def back_kernel(col0, where_ref, keep_ref, got_ref, far_ref, lat_ref, out_ref):
    cols = pl.ds(col0, got_ref.shape[1])
    extra = jnp.where(where_ref[1] == 0, keep_ref[:, cols], 0.0) + lat_ref[:, cols]
    out_ref[...] = before_sum(where_ref, got_ref, far_ref) + extra


def back_sum(where, after, keep, got, far, lat, col0=0):
    return call(
        lambda _, *refs: back_kernel(col0, *refs),
        (after, where, keep, got, far, lat),
        [ANY, SM] + [VM] * 4,
        [shaped(*got.shape)],
        (ROWS * HALF, 2000000, 0),
    )[0]


def base_kernel(
    where_ref, after_ref, anchor_ref, keep_ref, give_ref, beside_ref, got_ref, far_ref, own_ref, other_ref, back_ref
):
    core = where_ref[1]
    mine = pl.ds(pl.multiple_of(core * HALF, 128), HALF)
    other = pl.ds(pl.multiple_of((1 - core) * HALF, 128), HALF)
    before = before_sum(where_ref, got_ref, far_ref)
    own = before + jnp.where(core == 1, beside_ref[...], 0.0)
    own_ref[...] = anchor_ref[:, mine] + (keep_ref[...] + own)
    other_ref[...] = anchor_ref[:, other] + give_ref[...]
    back_ref[...] = before + jnp.where(core == 0, keep_ref[...], 0.0)


def base_sum(where, after, *terms):
    return call(
        base_kernel,
        (where, after, *terms),
        [SM, ANY] + [VM] * 6,
        [shaped(ROWS, HALF)] * 3,
        (ROWS * D * 2, 4000000, 0),
    )


def final_kernel(own, where_ref, *refs):
    core = where_ref[1]
    if own:
        _, base_ref, keep_ref, beside_ref, g0, g1, f0, f1, out_hbm, buf_ref, sems = refs
    else:
        _, base_ref, give_ref, b0, b1, out_hbm, buf_ref, sems = refs
    half = core if own else 1 - core
    copies = []
    for i in range(2):
        part = pl.ds(i * QUART, QUART)
        at = pl.ds(pl.multiple_of(half * HALF + i * QUART, 128), QUART)
        if own:
            got, far = ((g0, f0), (g1, f1))[i]
            more = before_sum(where_ref, got, far) + jnp.where(core == 1, beside_ref[:, part], 0.0)
            term = keep_ref[:, part] + more
        else:
            term = give_ref[:, part] + (b0, b1)[i][...]
        buf_ref[:, part] = base_ref[:, part] + term
        copies.append(pltpu.make_async_copy(buf_ref.at[:, part], out_hbm.at[:, at], sems.at[i]))
        copies[-1].start()
    for one in copies:
        one.wait()


def final_sum(own, args):
    n = len(args)
    return pl.pallas_call(
        functools.partial(final_kernel, own),
        in_specs=[SM, HBM if not own else ANY] + [VM] * (n - 2),
        out_specs=HBM,
        out_shape=shaped(ROWS, D),
        input_output_aliases={} if own else {1: 0},
        scratch_shapes=[pltpu.VMEM((ROWS, HALF), F32), pltpu.SemaphoreType.DMA((2,))],
        compiler_params=pltpu.CompilerParams(vmem_limit_bytes=24 << 20),
        cost_estimate=pl.CostEstimate(flops=ROWS * D, bytes_accessed=2000000, transcendentals=0),
        name="final_own" if own else "final_other",
    )(*args)


SWAP = pairs(lambda x, c, y, z: (x, 1 - c, y, z))
ROUND1 = pairs(lambda x, c, y, z: (x ^ 1, c, y, z))
ROUND2 = pairs(lambda x, c, y, z: (3 - x, c, y, z))


def held(x):
    return pltpu.with_memory_space_constraint(x, pltpu.HBM)


def per_device(iterate, anchor, frame_index, noise_steps, qkv_weight, out_weight, mod_weight):
    qkv_weight, mod_weight = held(qkv_weight), held(mod_weight)
    tm = lax.axis_index("tm")
    ctx = lax.axis_index("ctx")
    chip, core = tm // 2, tm % 2
    place = jnp.where(core == 0, ctx // 4, ctx % 4)
    where = jnp.stack([place, core, chip]).astype(jnp.int32)
    latent = held(iterate[0])
    rates = jnp.exp(-math.log(10000.0) * jnp.arange(128, dtype=F32) / 128)[None, :]
    frame_row = held(frame_index[None, :])

    tie = lax.optimization_barrier
    mine, latent, frame_row, features, gap = normed_pack(
        latent, frame_row, held(noise_steps), rates, mod_weight
    )
    from_prev = send(mine, exchange("a", 1))
    from_next = send(mine, exchange("a", 2))
    from_far = send(mine, along("a", 2))
    lat_keep, lat_give = lat_terms(where, latent, frame_row, gap)
    lat_beside = send(lat_give, SWAP)
    gate, weight = side_terms(
        where, lat_give, frame_row, gap, features, mod_weight, qkv_weight
    )
    (lat_both,) = add_up(lat_keep, lat_beside, F32, weight)
    lat_got = send(lat_both, ROUND1)

    q0, kv0 = project(mine, from_prev, weight, after=(lat_both,))
    up0 = send(kv0, exchange("b", 1))
    down0 = send(kv0, exchange("b", 2))
    q1, kv1 = project(from_next, from_far, weight, after=(kv0,))
    down1 = send(kv1, exchange("b", 2))
    up1 = send(kv1, exchange("b", 1))
    far0 = send(up0, exchange("b", 2))
    state = attend([kv0, kv1, up0, down0], queries=(q0, q1))
    down1_later, _ = tie((down1, state[1]))
    far1 = send(down1_later, exchange("b", 1))
    state = attend([up1, down1], state=state)
    (lat_wire,) = add_up(lat_both, lat_got, F32, state[1])
    a1, a2, a3 = attend([far0, far1], state=state, last=(ROWS, 3 * ROWS), after=(lat_wire,))
    lat_far = send(lat_wire, ROUND2)
    b3 = send(a3, along("a", 2))
    b1 = send(a1, exchange("a", 1))
    b2 = send(a2, exchange("a", 2))
    (a0,) = attend([far0, far1], state=state, last=(0, ROWS), after=(a1,))
    part = out_first(where, a0, out_weight)
    pieces = (b1, b2, b3)
    give = out_rest(False, where, part, part, pieces, out_weight, gate)
    beside = send(give, SWAP)
    keep = out_rest(True, where, give, part, pieces, out_weight, gate)
    both, wire0, wire1 = add_up(keep, beside, BF16, keep, n_parts=2, keep=True)
    got0 = send(wire0, ROUND1)
    got1 = send(wire1, ROUND1)
    pair0 = pair_up(0, both, got0, wire0)
    far0 = send(pair0, ROUND2)
    pair1 = pair_up(1, both, got1, pair0)
    far1 = send(pair1, ROUND2)
    base_own, base_other, lat_sum = base_sum(
        where, pair1, anchor, lat_keep, lat_give, lat_beside, lat_got, lat_far
    )
    sum0 = back_sum(where, pair1, keep, got0, far0, lat_sum)
    back0 = send(sum0, SWAP)
    sum1 = back_sum(where, sum0, keep, got1, far1, lat_sum, QUART)
    back1 = send(sum1, SWAP)
    out = final_sum(True, (where, sum1, base_own, keep, beside, got0, got1, far0, far1))
    out = final_sum(False, (where, out, base_other, give, back0, back1))
    return out[None]


def solution(mesh):
    placed = (P("tm", "ctx", None), P("ctx", None), P("ctx"), P("tm", None), P(), P(), P())

    return jax.shard_map(
        per_device, mesh=mesh, in_specs=placed, out_specs=P("tm", "ctx", None), check_vma=False
    )
```
